32 devices in a mesh: dp: 4 (over y, core), tm: 8 (over z, x).
Axes of the slice: x: 2, y: 2, z: 4, core: 2. Of those that a mesh axis runs over, the one named last changes fastest.
Arguments:
- features: bfloat16 [4, 16, 48, 48, 128], P('dp', 'tm'), may hold values from -6 to 6
- frame_counts: int32 [4, 6], P('dp'), may hold values from 1 to 8, 16 in all within a row
- conv1_weight: bfloat16 [3, 3, 3, 128, 128], replicated, may hold values from -0.109375 to 0.109375
- conv1_bias: float32 [128], replicated, may hold values from -3 to 3
- shrink_weight: bfloat16 [512, 128], replicated, may hold values from -0.25 to 0.25
- shrink_bias: float32 [128], replicated, may hold values from -3 to 3
- conv2_weight: bfloat16 [3, 3, 3, 128, 128], replicated, may hold values from -0.109375 to 0.109375
- conv2_bias: float32 [128], replicated, may hold values from -3 to 3
- embed_weight: bfloat16 [512, 1152], replicated, may hold values from -0.25 to 0.25
- embed_bias: float32 [1152], replicated, may hold values from -3 to 3
- bucket_table: float32 [8, 1152], replicated, may hold values from -5 to 5
- bucket_ids: int32 [4, 2304], P('dp', 'tm'), may hold values from 0 to 7
- dest_owner: int32 [4, 2304], P('dp', 'tm'), may hold values from 0 to 3, as said below
- dest_offset: int32 [4, 2304], P('dp', 'tm'), may hold values from 0 to 575, as said below
Outputs:
- packs: bfloat16 [4, 4608, 1152], P('dp', 'tm')
The draws below stay inside these ranges and needn't reach their ends.
Inputs may be any that keep to these rules, and one draw needn't show every extreme that they name: `dest_owner`: among the 288 rows of one device (r // 288 fixed) each owner is named at most 144 times; for each index of tm one owner is named exactly 144 times by every device of dp. `dest_offset`: the rows that share an owner and a value of r // 288 have distinct offsets.
All inputs are finite; a program needn't handle non-finite values.
Results may differ from the reference program's by a relative error of at most 0.0056.
Values may be sent and summed in bfloat16 or wider, within the bound.
A program may use at most 128 MiB of HBM per device.

```python
import math
import jax
import jax.numpy as jnp
import numpy as np
from jax import lax

C = 128
LAT = 1152
TAPS = 3
SIDE = 48
VIDS = 6
NB = 8
GROUPS = 4
FRAMES = 16
ROWS_DEV = 288
LROWS = 2304
CAP = 144
PACK = 576
SLOTS = 4608


def route_tables(key):
    column_count = LROWS // ROWS_DEV
    others = (GROUPS - 1) * CAP
    preference_key = jax.random.fold_in(key, 11)
    choose_key = jax.random.fold_in(key, 12)
    shuffle_key = jax.random.fold_in(key, 13)
    slot_key = jax.random.fold_in(key, 14)
    favoured = jax.random.randint(preference_key, (column_count,), 0, GROUPS).astype(jnp.int32)
    scores = jax.random.randint(choose_key, (GROUPS, column_count, others), 0, 1 << 20) * others + jnp.arange(others, dtype=jnp.int32)
    chosen = jnp.argsort(scores, axis=-1)[..., :ROWS_DEV - CAP].astype(jnp.int32)
    owners_rest = chosen // CAP
    favour_wide = favoured[None, :, None]
    owners_rest = owners_rest + (owners_rest >= favour_wide).astype(jnp.int32)
    owners = jnp.concatenate([jnp.broadcast_to(favour_wide, (GROUPS, column_count, CAP)), owners_rest], axis=-1)
    shuffle_scores = jax.random.randint(shuffle_key, (GROUPS, column_count, ROWS_DEV), 0, 1 << 20) * ROWS_DEV + jnp.arange(ROWS_DEV, dtype=jnp.int32)
    owners = jnp.take_along_axis(owners, jnp.argsort(shuffle_scores, axis=-1), axis=-1).astype(jnp.int32)
    match_flags = (owners[..., None] == jnp.arange(GROUPS, dtype=jnp.int32)).astype(jnp.int32)
    position = jnp.sum((jnp.cumsum(match_flags, axis=2) - 1) * match_flags, axis=-1)
    slot_scores = jax.random.randint(slot_key, (GROUPS, column_count, PACK), 0, 1 << 20) * PACK + jnp.arange(PACK, dtype=jnp.int32)
    slot_table = jnp.argsort(slot_scores, axis=-1).astype(jnp.int32)
    sources = jnp.arange(GROUPS, dtype=jnp.int32)[:, None, None]
    columns = jnp.arange(column_count, dtype=jnp.int32)[None, :, None]
    offsets = slot_table[owners, columns, sources * CAP + position]
    return (owners.reshape(GROUPS, LROWS), offsets.reshape(GROUPS, LROWS).astype(jnp.int32))


def draw_dest_owner(key, part):
    return route_tables(jax.random.fold_in(key, 7))[0]


def draw_dest_offset(key, part):
    return route_tables(jax.random.fold_in(key, 7))[1]


def with_ends(result, rng, least, largest):
    spot = [jax.random.randint(jax.random.fold_in(rng, axis), (), 0, length) for axis, length in enumerate(result.shape)]
    widest = result.shape.index(max(result.shape))
    next_to = spot[:widest] + [(spot[widest] + 1) % result.shape[widest]] + spot[widest + 1:]
    return result.at[tuple(spot)].set(least).at[tuple(next_to)].set(largest)


def level_of(own_key, dims, split, least, top_value):
    loudness = 1.0
    for axis_at, blocks in split:
        steps = jax.random.uniform(jax.random.fold_in(jax.random.fold_in(own_key, 6), axis_at), (blocks,), jnp.float32, least / len(split), top_value / len(split))
        loudness = loudness * jnp.repeat(jnp.exp(steps), dims[axis_at] // blocks).reshape((-1,) + (1,) * (len(dims) - 1 - axis_at))
    return loudness


def split_up(number_of, total, limit, skew):
    weights = [(1 << 20) // math.isqrt(standing ** skew) + 1 for standing in range(2, number_of + 1)]
    surplus, holding = total - limit - (number_of - 1), [1] * (number_of - 1)
    while surplus > 0:
        movable = [i for i in range(number_of - 1) if holding[i] < limit]
        whole, remaining = sum([weights[i] for i in movable]), surplus
        for i in movable:
            more = min(limit - holding[i], max(1, remaining * weights[i] // whole), surplus)
            holding[i] = holding[i] + more
            surplus = surplus - more
    return np.array([limit] + holding)


def ragged_sizes(own_key, number_of, total, reach, lean):
    if number_of == 2:
        one = jax.random.randint(own_key, (), max(1, total - reach), min(reach, total - 1) + 1)
        return jnp.stack([one, total - one])
    tallies = jnp.asarray(split_up(number_of, total, reach, lean), jnp.int32)
    couples = (number_of - 1) // 2
    source_of, receiver = tallies[1:1 + 2 * couples:2], tallies[2:2 + 2 * couples:2]
    margin = jnp.minimum(source_of - 1, reach - receiver)
    moved = jax.random.randint(jax.random.fold_in(own_key, 1), (couples,), 0, 1 << 20) % (margin + 1)
    tallies = tallies.at[1:1 + 2 * couples:2].set(source_of - moved).at[2:2 + 2 * couples:2].set(receiver + moved)
    return tallies[jax.random.permutation(jax.random.fold_in(own_key, 2), number_of)]


def gaussian(rng, extent, scale, most, cuts=(), kind=jnp.bfloat16):
    loudness = level_of(rng, extent, cuts, -0.22, 0.18) if cuts else 1.0
    values = jax.random.normal(rng, extent, jnp.float32) * scale * loudness
    return jnp.minimum(jnp.maximum(values, -most), most).astype(kind)


def setup_inputs(seed: int = 0) -> dict:
    keys = jax.random.split(jax.random.key(seed), 15)
    return {
        "features": gaussian(keys[0], (GROUPS, FRAMES, SIDE, SIDE, C), 1.0, 6.0, ((0, 4), (1, 8))),
        "frame_counts": jax.vmap(lambda own: ragged_sizes(own, VIDS, FRAMES, FRAMES // 2, 2))(jax.random.split(keys[1], GROUPS)).reshape((GROUPS, VIDS)).astype(jnp.int32),
        "conv1_weight": gaussian(keys[2], (TAPS, 3, 3, C, C), (TAPS * 9 * C) ** -0.5, 0.109375),
        "conv1_bias": gaussian(keys[3], (C,), 0.5, 3.0, (), jnp.float32),
        "shrink_weight": gaussian(keys[4], (4 * C, C), (4 * C) ** -0.5, 0.25),
        "shrink_bias": gaussian(keys[5], (C,), 0.5, 3.0, (), jnp.float32),
        "conv2_weight": gaussian(keys[6], (TAPS, 3, 3, C, C), (TAPS * 9 * C) ** -0.5, 0.109375),
        "conv2_bias": gaussian(keys[7], (C,), 0.5, 3.0, (), jnp.float32),
        "embed_weight": gaussian(keys[8], (4 * C, LAT), (4 * C) ** -0.5, 0.25),
        "embed_bias": gaussian(keys[9], (LAT,), 0.5, 3.0, (), jnp.float32),
        "bucket_table": gaussian(keys[10], (NB, LAT), 1.0, 5.0, (), jnp.float32),
        "bucket_ids": with_ends(jax.random.randint(keys[11], (GROUPS, LROWS), 0, NB), jax.random.fold_in(keys[11], 1), 0, NB - 1).astype(jnp.int32),
        "dest_owner": draw_dest_owner(jax.random.fold_in(keys[14], 71), 0),
        "dest_offset": draw_dest_offset(jax.random.fold_in(keys[14], 71), 0),
    }


def frame_masks(counts, first_frame, length):
    frames = first_frame + jnp.arange(length, dtype=jnp.int32)
    bounds = jnp.cumsum(counts).astype(jnp.int32)

    def segment(moments):
        return jnp.sum((moments[:, None] >= bounds[None, :]).astype(jnp.int32), axis=1)

    current = segment(frames)
    columns = []
    for distance in (2, 1):
        earlier = frames - distance
        columns.append(((earlier >= 0) & (segment(earlier) == current)).astype(jnp.float32))
    return jnp.stack(columns, axis=1)


def causal_conv(window, valid, kernel, conv_bias):
    outputs = valid.shape[0]
    side = window.shape[1]
    channels = window.shape[3]
    nothing = jnp.zeros((), window.dtype)
    oldest = jnp.where(valid[:, 0, None, None, None] > 0, window[0:outputs], nothing)
    middle = jnp.where(valid[:, 1, None, None, None] > 0, window[1:outputs + 1], nothing)
    stacked = jnp.concatenate([oldest, middle, window[2:outputs + 2]], axis=-1)
    padded = jnp.pad(stacked, ((0, 0), (1, 1), (1, 1), (0, 0)))
    taps_all = kernel.transpose(1, 2, 0, 3, 4).reshape(3, 3, 3 * channels, channels)
    total = jnp.zeros((outputs * side * side, channels), jnp.float32)
    for row_step in range(3):
        for col_step in range(3):
            piece = padded[:, row_step:row_step + side, col_step:col_step + side, :].reshape(-1, 3 * channels)
            total = total + jnp.dot(piece, taps_all[row_step, col_step], preferred_element_type=jnp.float32)
    return total.reshape(outputs, side, side, channels) + conv_bias


def fold_blocks(receptive_field):
    frame_total = receptive_field.shape[0]
    side = receptive_field.shape[1]
    channels = receptive_field.shape[3]
    blocks = receptive_field.reshape(frame_total, side // 2, 2, side // 2, 2, channels).transpose(0, 1, 3, 2, 4, 5)
    return blocks.reshape(frame_total, side // 2, side // 2, 4 * channels)


def residual_section(window, valid, kernel, conv_bias, inputs):
    return (inputs.astype(jnp.float32) + jax.nn.silu(causal_conv(window, valid, kernel, conv_bias))).astype(jnp.bfloat16)


def spatial_shrink(receptive_field, shrink_weight, shrink_bias):
    folded = fold_blocks(receptive_field)
    shape_out = folded.shape[:3] + (shrink_weight.shape[1],)
    mixed = jnp.dot(folded.reshape(-1, folded.shape[3]), shrink_weight, preferred_element_type=jnp.float32) + shrink_bias
    return mixed.astype(jnp.bfloat16).reshape(shape_out)


def reference(features, frame_counts, conv1_weight, conv1_bias, shrink_weight, shrink_bias, conv2_weight, conv2_bias, embed_weight, embed_bias, bucket_table, bucket_ids, dest_owner, dest_offset):
    def one_row(inputs):
        slab, counts, buckets = inputs
        valid = frame_masks(counts, jnp.int32(0), FRAMES)
        padding = jnp.zeros((2,) + slab.shape[1:], slab.dtype)
        section_first = residual_section(jnp.concatenate([padding, slab], axis=0), valid, conv1_weight, conv1_bias, slab)
        reduced_result = spatial_shrink(section_first, shrink_weight, shrink_bias)
        padding_two = jnp.zeros((2,) + reduced_result.shape[1:], reduced_result.dtype)
        section_two = residual_section(jnp.concatenate([padding_two, reduced_result], axis=0), valid, conv2_weight, conv2_bias, reduced_result)
        patches = fold_blocks(section_two).reshape(-1, 4 * section_two.shape[3])
        latent = jnp.dot(patches, embed_weight, preferred_element_type=jnp.float32) + embed_bias + bucket_table[buckets]
        return latent.astype(jnp.bfloat16)

    latents = lax.map(one_row, (features, frame_counts, bucket_ids))
    column_count = LROWS // ROWS_DEV
    columns = jnp.arange(LROWS, dtype=jnp.int32) // ROWS_DEV
    flat = dest_owner * (column_count * PACK) + columns[None, :] * PACK + dest_offset
    packs = jnp.zeros((GROUPS * column_count * PACK, LAT), jnp.bfloat16)
    packs = packs.at[flat.reshape(-1)].set(latents.reshape(-1, LAT))
    return packs.reshape(GROUPS, SLOTS, LAT)
```

```python
import functools
import jax
import jax.numpy as jnp
from jax import lax
from jax.experimental import pallas as pl
from jax.experimental.pallas import tpu as pltpu
from jax.sharding import PartitionSpec as P

MESH = pl.DeviceIdType.MESH
F32 = jnp.float32
BF16 = jnp.bfloat16
SIDE = 48
HALF = SIDE // 2
PAD = 8
STEPS = 12
LOTS = 6
LAG = 3
KEEP = 9
LEAD = 3


def silu(v):
    return v / (1.0 + jnp.exp(-v))


def span(i):
    return (0, 6) if i == 0 else (4 * i + 2, 2 if i == STEPS - 1 else 4)


def live_factors(counts, first, videos):
    def segment(moment):
        at = moment.astype(F32)
        total = jnp.zeros((1, 1), F32)
        bound = jnp.zeros((1, 1), F32)
        for i in range(videos):
            bound = bound + counts[0:1, i : i + 1]
            total = total + jnp.where(at >= bound, 1.0, 0.0)
        return total

    seg = {d: segment(first + d) for d in (-2, -1, 0, 1)}

    def live(frame, distance):
        same = jnp.where(seg[frame] == seg[frame - distance], 1.0, 0.0)
        there = jnp.where(first + frame - distance >= 0, 1.0, 0.0).astype(F32)
        return jnp.broadcast_to(same * there, (1, 128)).astype(BF16)

    return live


def body(
    rows,
    pack,
    n_tm,
    n_dp,
    videos,
    names,
    feat,
    counts_in,
    w1_in,
    b1_in,
    sw_in,
    sb_in,
    w2_in,
    b2_in,
    bucket_in,
    owner_in,
    offset_in,
    out,
    raw,
    p1,
    p2,
    w1,
    w2,
    sw,
    counts,
    b1,
    sb,
    b2,
    bucket,
    owner,
    offset,
    wm1,
    wm2,
    cnt,
    rsend,
    rrecv,
    fs,
    stage,
    psend,
    patches,
    meta,
    metas,
    hot,
    got,
    outv,
    load_sem,
    own_sem,
    out_sem,
    csend_sem,
    crecv_sem,
    xsend_sem,
    xrecv_sem,
    nsend_sem,
    nrecv_sem,
    fsend_sem,
    frecv_sem,
    rsend_sem,
    rrecv_sem,
    gsend_sem,
    grecv_sem,
    psend_sem,
    precv_sem,
    msend_sem,
    mrecv_sem,
):
    dp = lax.axis_index("dp")
    tm = lax.axis_index("tm")
    core = lax.rem(dp, 2)
    side = lax.rem(tm, 2)
    late = core == side
    early = core != side
    twin = dp + 1 - 2 * core
    across = (dp, tm + 1 - 2 * side)
    late_at = late.astype(jnp.int32)
    ahead = (twin, lax.rem(tm + 2 * late_at, n_tm))
    above = (twin, lax.rem(tm + 2, n_tm))
    below = (twin, lax.rem(tm + n_tm - 2, n_tm))
    row = dp - core + side
    slab = tm - side + late_at
    up = late & (tm < n_tm - 2)
    down = early & (tm > 1)
    lift = early & (side == 1) & (tm < n_tm - 2)
    land = down & (side == 0)
    lift_to = (twin, lax.rem(tm + 1, n_tm))
    land_from = (twin, lax.rem(tm + n_tm - 1, n_tm))
    has_next = early | up
    has_prev = late | down
    pairs = n_dp // 2
    home = dp - core + lax.rem(side + core + 1, 2)
    lot = 2 * HALF

    loads = [
        pltpu.make_async_copy(src, dst, load_sem.at[i])
        for i, (src, dst) in enumerate(
            (
                (counts_in, counts),
                (owner_in, owner),
                (offset_in, offset),
                (bucket_in, bucket),
                (w1_in, w1),
                (w2_in, w2),
                (sw_in, sw),
                (b1_in, b1),
                (sb_in, sb),
                (b2_in, b2),
            )
        )
    ]
    load_own = pltpu.make_async_copy(feat.at[0], raw.at[side], own_sem)

    barrier = pltpu.get_barrier_semaphore()
    for k in range(1, n_dp):
        pl.semaphore_signal(
            barrier, inc=1, device_id=(lax.rem(dp + k, n_dp), tm), device_id_type=MESH
        )

    pl.semaphore_signal(barrier, inc=1, device_id=across, device_id_type=MESH)

    @pl.when(up)
    def _():
        pl.semaphore_signal(barrier, inc=1, device_id=above, device_id_type=MESH)

    @pl.when(down)
    def _():
        pl.semaphore_signal(barrier, inc=1, device_id=below, device_id_type=MESH)

    @pl.when(lift)
    def _():
        pl.semaphore_signal(barrier, inc=1, device_id=lift_to, device_id_type=MESH)

    @pl.when(land)
    def _():
        pl.semaphore_signal(barrier, inc=1, device_id=land_from, device_id_type=MESH)

    for load in loads:
        load.start()
    links = sum(flag.astype(jnp.int32) for flag in (up, down, lift, land))
    pl.semaphore_wait(barrier, n_dp + links)

    def cross_copy(y0, n, i):
        return pltpu.make_async_remote_copy(
            src_ref=feat.at[0, :, pl.ds(y0, n)],
            dst_ref=raw.at[side, :, pl.ds(y0, n)],
            send_sem=xsend_sem.at[i],
            recv_sem=xrecv_sem.at[i],
            device_id=across,
            device_id_type=MESH,
        )

    def near_copy(src, y0, n, i):
        return pltpu.make_async_remote_copy(
            src_ref=src.at[:, pl.ds(y0, n)],
            dst_ref=raw.at[1, :, pl.ds(y0, n)],
            send_sem=nsend_sem.at[i],
            recv_sem=nrecv_sem.at[i],
            device_id=(twin, tm),
            device_id_type=MESH,
        )

    def far_copy(src, y0, n, i):
        return pltpu.make_async_remote_copy(
            src_ref=src.at[:, pl.ds(y0, n)],
            dst_ref=raw.at[0, :, pl.ds(y0, n)],
            send_sem=fsend_sem.at[i],
            recv_sem=frecv_sem.at[i],
            device_id=above,
            device_id_type=MESH,
        )

    def lift_copy(y0, n, i):
        return pltpu.make_async_remote_copy(
            src_ref=feat.at[0, :, pl.ds(y0, n)],
            dst_ref=raw.at[0, :, pl.ds(y0, n)],
            send_sem=fsend_sem.at[i],
            recv_sem=frecv_sem.at[i],
            device_id=lift_to,
            device_id_type=MESH,
        )

    def count_copy():
        return pltpu.make_async_remote_copy(
            src_ref=cnt.at[0],
            dst_ref=cnt.at[1],
            send_sem=csend_sem,
            recv_sem=crecv_sem,
            device_id=(twin, tm),
            device_id_type=MESH,
        )

    def red_copy(i):
        at = pl.ds(pl.multiple_of(i * 96, 96), 96)
        return pltpu.make_async_remote_copy(
            src_ref=rsend.at[at],
            dst_ref=rrecv.at[at],
            send_sem=rsend_sem.at[i],
            recv_sem=rrecv_sem.at[i],
            device_id=ahead,
            device_id_type=MESH,
        )

    def slot_of(d):
        return pl.ds(pl.multiple_of(d * lot, lot), lot)

    def home_copy(j):
        return pltpu.make_async_remote_copy(
            src_ref=psend.at[j],
            dst_ref=patches.at[j, slot_of(row)],
            send_sem=gsend_sem.at[j],
            recv_sem=grecv_sem.at[j],
            device_id=across,
            device_id_type=MESH,
        )

    def share_copy(j, k):
        at = slot_of(home)
        return pltpu.make_async_remote_copy(
            src_ref=patches.at[j, at],
            dst_ref=patches.at[j, at],
            send_sem=psend_sem.at[j, k],
            recv_sem=precv_sem.at[j, k],
            device_id=(lax.rem(dp + 2 * k, n_dp) if k else twin, tm),
            device_id_type=MESH,
        )

    def pass_copy(j, k):
        at = slot_of(lax.rem(home + n_dp - 2 * k, n_dp))
        return pltpu.make_async_remote_copy(
            src_ref=patches.at[j, at],
            dst_ref=patches.at[j, at],
            send_sem=psend_sem.at[j, pairs + k],
            recv_sem=precv_sem.at[j, pairs + k],
            device_id=(twin, tm),
            device_id_type=MESH,
        )

    def meta_copy(k):
        return pltpu.make_async_remote_copy(
            src_ref=meta,
            dst_ref=metas.at[dp],
            send_sem=msend_sem.at[k],
            recv_sem=mrecv_sem.at[k],
            device_id=(lax.rem(dp + k, n_dp), tm),
            device_id_type=MESH,
        )

    @pl.when(early)
    def _():
        for i in range(STEPS):
            cross_copy(*span(i), i).start()

    @pl.when(lift)
    def _():
        for i in range(KEEP, STEPS):
            lift_copy(*span(i), i).start()

    @pl.when(late)
    def _():
        load_own.start()

        @pl.when(side == 0)
        def _():
            for i in range(STEPS):
                near_copy(feat.at[0], *span(i), i).start()

        @pl.when((side == 1) & up)
        def _():
            for i in range(LEAD):
                far_copy(feat.at[0], *span(i), i).start()

    loads[0].wait()
    cnt[0] = jnp.zeros((8, 128), F32)
    cnt[0, 0:1, 0:videos] = counts[...].astype(F32)

    @pl.when(late)
    def _():
        count_copy().start()

    for load in loads[1:4]:
        load.wait()
    code = (owner[...] * pack + offset[...] + 1).astype(F32)
    named = jnp.concatenate(
        [code, bucket[...].astype(F32), jnp.zeros((6, rows), F32)], axis=0
    )
    frame = rows // 2
    meta[...] = jnp.concatenate(
        [
            named[:, f * frame + j * HALF : f * frame + j * HALF + HALF]
            for j in range(LOTS)
            for f in range(2)
        ],
        axis=1,
    )
    metas[dp] = meta[...]
    for k in range(1, n_dp):
        meta_copy(k).start()

    for field, side_len in ((p1, SIDE), (p2, HALF)):
        wide = field.shape[2]
        for s in range(4):
            field[s, :, 0:PAD] = jnp.zeros((side_len + 2, PAD, 128), F32)
            field[s, :, PAD + side_len : wide] = jnp.zeros((side_len + 2, PAD, 128), F32)
            field[s, 0] = jnp.zeros((wide, 128), F32)
            field[s, side_len + 1] = jnp.zeros((wide, 128), F32)

    @pl.when(jnp.logical_not(has_prev))
    def _():
        p1[0:2] = jnp.zeros((2,) + p1.shape[1:], F32)
        p2[0:2] = jnp.zeros((2,) + p2.shape[1:], F32)

    @pl.when(early)
    def _():
        count_copy().wait_recv()

    @pl.when(late)
    def _():
        cnt[1] = cnt[0]

    live = live_factors(cnt[1], slab * 2, videos)
    for load in loads[4:]:
        load.wait()
    for w, wm in ((w1, wm1), (w2, wm2)):
        wm[0, :, 0:128] = w[0] * live(0, 2)
        wm[1, :, 0:128] = w[1] * live(0, 1)
        wm[1, :, 128:256] = w[0] * live(1, 2)
        wm[2, :, 0:128] = w[2]
        wm[2, :, 128:256] = w[1] * live(1, 1)

    def mm(a, w):
        return jnp.dot(a, w, preferred_element_type=F32)

    def widen(pair, y0, n):
        for f in range(2):
            p1[2 * pair + f, pl.ds(1 + y0, n), PAD : PAD + SIDE, :] = raw[
                pair, f, pl.ds(y0, n)
            ].astype(F32)

    def take(y0, n, i):
        @pl.when(late)
        def _():
            cross_copy(y0, n, i).wait_recv()

            @pl.when((side == 0) & up & (i < KEEP))
            def _():
                far_copy(raw.at[1], y0, n, i).start()

            @pl.when(side == 1)
            def _():
                near_copy(raw.at[0], y0, n, i).start()

        @pl.when(early)
        def _():
            near_copy(raw.at[1], y0, n, i).wait_recv()

        @pl.when(down)
        def _():
            far_copy(raw.at[0], y0, n, i).wait_recv()

        widen(1, y0, n)

        @pl.when(has_prev)
        def _():
            widen(0, y0, n)

    def field1(s, y0):
        sides = []
        for parity in range(2):
            parts = []
            for dy in range(3):
                for dx in range(3):
                    v = p1[s, pl.ds(y0 + dy, 4), pl.ds(PAD + parity + dx - 1, 24, stride=2), :]
                    parts.append(v.reshape(96, 128).astype(BF16))
            sides.append(jnp.concatenate(parts, axis=1))
        return jnp.concatenate(sides, axis=0)

    def field2(s, y0):
        parts = []
        for dy in range(3):
            for dx in range(3):
                v = p2[s, pl.ds(y0 + dy, 4), PAD + dx - 1 : PAD + dx + 23, :]
                parts.append(v.reshape(96, 128).astype(BF16))
        return jnp.concatenate(parts, axis=1)

    def conv(field, y0, wm, w):
        both = mm(field(1, y0), wm[1]) + mm(field(2, y0), wm[2])
        ends = (mm(field(0, y0), wm[0, :, 0:128]), mm(field(3, y0), w[2]))
        return [both[:, f * 128 : f * 128 + 128] + ends[f] for f in range(2)]

    def section_one(i):
        y0 = 4 * i
        zs = conv(field1, y0, wm1, w1)
        blocks = []
        for f in range(2):
            z = (zs[f] + b1[...]).reshape(2, 2, 2, 24, 128)
            parts = {}
            for parity in range(2):
                x = p1[2 + f, pl.ds(1 + y0, 4), pl.ds(PAD + parity, 24, stride=2), :]
                x = x.reshape(2, 2, 24, 128)
                for by in range(2):
                    parts[by, parity] = (
                        (x[:, by] + silu(z[parity, :, by])).reshape(48, 128).astype(BF16)
                    )
            blocks.append(
                jnp.concatenate(
                    [parts[by, parity] for by in range(2) for parity in range(2)], axis=1
                )
            )
        red = (mm(jnp.concatenate(blocks, axis=0), sw[...]) + sb[...]).astype(BF16)
        rsend[pl.ds(pl.multiple_of(i * 96, 96), 96), :] = red

        @pl.when(has_next)
        def _():
            red_copy(i).start()

        wide = red.astype(F32).reshape(2, 2, 24, 128)
        for f in range(2):
            p2[2 + f, pl.ds(1 + 2 * i, 2), PAD : PAD + HALF, :] = wide[f]

    def take_red(i):
        red_copy(i).wait_recv()
        wide = rrecv[pl.ds(pl.multiple_of(i * 96, 96), 96), :].astype(F32)
        wide = wide.reshape(2, 2, 24, 128)
        for f in range(2):
            p2[f, pl.ds(1 + 2 * i, 2), PAD : PAD + HALF, :] = wide[f]

    def section_two(j):
        @pl.when(has_prev)
        def _():
            @pl.when(j == 0)
            def _():
                take_red(0)

            take_red(2 * j + 1)

            @pl.when(j < LOTS - 1)
            def _():
                take_red(2 * j + 2)

        y0 = 4 * j
        zs = conv(field2, y0, wm2, w2)
        for f in range(2):
            x = p2[2 + f, pl.ds(1 + y0, 4), PAD : PAD + HALF, :].reshape(96, 128)
            fs[f] = x + silu(zs[f] + b2[...])
            for b in range(2):
                for by in range(2):
                    for bx in range(2):
                        lane = (by * 2 + bx) * 128
                        to = f * 24 + b * 12
                        stage[to : to + 12, lane : lane + 128] = fs[
                            f, pl.ds(48 * b + 24 * by + bx, 12, stride=2), :
                        ]
        done = stage[...].astype(BF16)

        @pl.when(core == 0)
        def _():
            psend[j] = done
            home_copy(j).start()

        @pl.when(core == 1)
        def _():
            patches[j, slot_of(home), :] = done

    def share(j):
        @pl.when(core == 0)
        def _():
            home_copy(j).wait_recv()

        for k in range(pairs):
            share_copy(j, k).start()

    def hand_on(j):
        for k in range(1, pairs):
            share_copy(j, k).wait_recv()
            pass_copy(j, k).start()

    def prepare():
        for k in range(1, n_dp):
            meta_copy(k).wait_recv()
        slot = lax.broadcasted_iota(jnp.int32, (pack, n_dp * lot), 0) + (dp * pack + 1)
        slot = slot.astype(F32)
        at = lax.broadcasted_iota(jnp.int32, (128, n_dp * lot), 0)
        name = lax.rem(at, names).astype(F32)
        inside = at < 3 * names
        sel = jnp.zeros((pack, 128), F32)
        for j in range(LOTS):
            both = jnp.concatenate(
                [metas[d, :, j * lot : j * lot + lot] for d in range(n_dp)], axis=1
            )
            marks = jnp.where(slot == both[0:1], 1.0, 0.0).astype(BF16)
            hot[j] = marks
            chosen = jnp.where((name == both[1:2]) & inside, 1.0, 0.0).astype(BF16)
            sel = sel + lax.dot_general(
                marks, chosen, (((1,), (1,)), ((), ())), preferred_element_type=F32
            )
        outv[:, 512:640] = sel.astype(BF16)

    @pl.when(late)
    def _():
        load_own.wait()

    first = core * (1 - side)
    burst = (1 - core) * (1 - side)
    share_at = 3 * first + (STEPS + 1) * burst + 9 * side
    share_by = 2 - burst
    pass_at = 20 - 13 * first
    pass_by = 1 + first

    def advance(s, carry):
        @pl.when(s < STEPS)
        def _():
            @pl.when(s == 0)
            def _():
                take(*span(0), 0)

            @pl.when((s > 0) & (s < STEPS - 1))
            def _():
                take(4 * s + 2, 4, s)

            @pl.when(s == STEPS - 1)
            def _():
                take(*span(STEPS - 1), STEPS - 1)

            section_one(s)

        @pl.when(s == STEPS * late_at)
        def _():
            prepare()

        def turn(start, by, fn):
            t = s - start
            ready = (t >= 0) & (t < by * LOTS) & (lax.rem(t + 2 * STEPS * by, by) == 0)

            @pl.when(ready)
            def _():
                fn(t // by)

        @pl.when((side == 1) & up)
        def _():
            @pl.when(s < STEPS - 1 - LEAD)
            def _():
                far_copy(feat.at[0], 4 * (s + LEAD) + 2, 4, s + LEAD).start()

            @pl.when(s == STEPS - 1 - LEAD)
            def _():
                far_copy(feat.at[0], *span(STEPS - 1), STEPS - 1).start()

        turn(2 + 2 * LAG * late_at, 2, section_two)
        turn(share_at, share_by, share)
        turn(pass_at, pass_by, hand_on)
        return carry

    lax.fori_loop(0, 26, advance, 0)

    def arrive(j):
        share_copy(j, 0).wait_recv()
        for k in range(1, pairs):
            pass_copy(j, k).wait_recv()

    for j in range(LOTS - 1):
        arrive(j)
    total = mm(hot[0], patches[0])
    for j in range(1, LOTS - 1):
        total = total + mm(hot[j], patches[j])
    got[...] = total
    arrive(LOTS - 1)
    tile = pack // 2
    stores = []
    for m in range(2):
        at = pl.ds(m * tile, tile)
        rest = got[at] + mm(hot[LOTS - 1, at], patches[LOTS - 1])
        outv[at, 0:512] = rest.astype(BF16)
        stores.append(pltpu.make_async_copy(outv.at[at], out.at[at], out_sem.at[m]))
        stores[m].start()

    @pl.when(early)
    def _():
        for i in range(STEPS):
            cross_copy(*span(i), i).wait_send()

    @pl.when(late)
    def _():
        count_copy().wait_send()
        for i in range(STEPS):
            near_copy(raw.at[0], *span(i), i).wait_send()

    @pl.when(up)
    def _():
        for i in range(KEEP):
            far_copy(raw.at[1], *span(i), i).wait_send()

    @pl.when((up & (side == 1)) | lift)
    def _():
        for i in range(KEEP, STEPS):
            far_copy(raw.at[1], *span(i), i).wait_send()

    @pl.when(core == 0)
    def _():
        for j in range(LOTS):
            home_copy(j).wait_send()

    @pl.when(has_next)
    def _():
        for i in range(STEPS):
            red_copy(i).wait_send()

    for k in range(1, n_dp):
        meta_copy(k).wait_send()
    for j in range(LOTS):
        share_copy(j, 0).wait_send()
        for k in range(1, pairs):
            share_copy(j, k).wait_send()
            pass_copy(j, k).wait_send()
    for store in stores:
        store.wait()


def embed(packed, ew, eb, table, out):
    names = table.shape[0]
    full = table[...] + eb[...].reshape(1, -1)
    high = full.astype(BF16).astype(F32)
    mid = (full - high).astype(BF16).astype(F32)
    low = full - high - mid
    split = jnp.concatenate(
        [high, mid, low, jnp.zeros((128 - 3 * names, full.shape[1]), F32)], axis=0
    ).astype(BF16)
    total = jnp.dot(packed[:, 0:512], ew[...], preferred_element_type=F32)
    total = total + jnp.dot(packed[:, 512:640], split, preferred_element_type=F32)
    out[...] = total.astype(BF16)


def shards(
    n_dp,
    n_tm,
    features,
    frame_counts,
    conv1_weight,
    conv1_bias,
    shrink_weight,
    shrink_bias,
    conv2_weight,
    conv2_bias,
    embed_weight,
    embed_bias,
    bucket_table,
    bucket_ids,
    dest_owner,
    dest_offset,
):
    rows = dest_owner.shape[1]
    pack = 2 * rows
    lat = embed_weight.shape[1]
    videos = frame_counts.shape[1]
    anywhere = pl.BlockSpec(memory_space=pl.ANY)
    pairs = n_dp // 2
    lot = 2 * HALF
    dma = pltpu.SemaphoreType.DMA
    gathered = pl.pallas_call(
        functools.partial(body, rows, pack, n_tm, n_dp, videos, bucket_table.shape[0]),
        out_shape=pltpu.VMEM((pack, 640), BF16),
        in_specs=[anywhere] * 11,
        out_specs=anywhere,
        scratch_shapes=[
            pltpu.VMEM((2, 2, SIDE, SIDE, 128), BF16),
            pltpu.VMEM((4, SIDE + 2, SIDE + 2 * PAD, 128), F32),
            pltpu.VMEM((4, HALF + 2, HALF + 2 * PAD, 128), F32),
            pltpu.VMEM((3, 1152, 128), BF16),
            pltpu.VMEM((3, 1152, 128), BF16),
            pltpu.VMEM((512, 128), BF16),
            pltpu.VMEM((1, videos), jnp.int32),
            pltpu.VMEM((1, 128), F32),
            pltpu.VMEM((1, 128), F32),
            pltpu.VMEM((1, 128), F32),
            pltpu.VMEM((1, rows), jnp.int32),
            pltpu.VMEM((1, rows), jnp.int32),
            pltpu.VMEM((1, rows), jnp.int32),
            pltpu.VMEM((3, 1152, 256), BF16),
            pltpu.VMEM((3, 1152, 256), BF16),
            pltpu.VMEM((2, 8, 128), F32),
            pltpu.VMEM((STEPS * 96, 128), BF16),
            pltpu.VMEM((STEPS * 96, 128), BF16),
            pltpu.VMEM((2, 96, 128), F32),
            pltpu.VMEM((lot, 512), F32),
            pltpu.VMEM((LOTS, lot, 512), BF16),
            pltpu.VMEM((LOTS, n_dp * lot, 512), BF16),
            pltpu.VMEM((8, rows), F32),
            pltpu.VMEM((n_dp, 8, rows), F32),
            pltpu.VMEM((LOTS, pack, n_dp * lot), BF16),
            pltpu.VMEM((pack, 512), F32),
            pltpu.VMEM((pack, 640), BF16),
            dma((10,)),
            dma,
            dma((2,)),
            dma,
            dma,
            dma((STEPS,)),
            dma((STEPS,)),
            dma((STEPS,)),
            dma((STEPS,)),
            dma((STEPS,)),
            dma((STEPS,)),
            dma((STEPS,)),
            dma((STEPS,)),
            dma((LOTS,)),
            dma((LOTS,)),
            dma((LOTS, 2 * pairs)),
            dma((LOTS, 2 * pairs)),
            dma((n_dp,)),
            dma((n_dp,)),
        ],
        compiler_params=pltpu.CompilerParams(
            collective_id=0, has_side_effects=True, vmem_limit_bytes=56 * 1024 * 1024
        ),
        name="encoder",
    )(
        features,
        frame_counts,
        conv1_weight.reshape(3, 1152, 128),
        conv1_bias.reshape(1, 128),
        shrink_weight,
        shrink_bias.reshape(1, 128),
        conv2_weight.reshape(3, 1152, 128),
        conv2_bias.reshape(1, 128),
        bucket_ids,
        dest_owner,
        dest_offset,
    )
    tile = pack // 2
    packed = pl.pallas_call(
        embed,
        grid=(2,),
        out_shape=jax.ShapeDtypeStruct((pack, lat), BF16),
        in_specs=[
            pl.BlockSpec((tile, 640), lambda i: (i, 0)),
            pl.BlockSpec((512, lat), lambda i: (0, 0)),
            pl.BlockSpec((lat,), lambda i: (0,)),
            pl.BlockSpec(bucket_table.shape, lambda i: (0, 0)),
        ],
        out_specs=pl.BlockSpec((tile, lat), lambda i: (i, 0)),
        compiler_params=pltpu.CompilerParams(vmem_limit_bytes=48 * 1024 * 1024),
        name="embed",
    )(gathered, embed_weight, embed_bias, bucket_table)
    return packed[None]


def solution(mesh):
    sizes = dict(mesh.shape)
    return jax.shard_map(
        functools.partial(shards, sizes["dp"], sizes["tm"]),
        mesh=mesh,
        in_specs=(
            P("dp", "tm", None, None, None),
            P("dp", None),
            P(),
            P(),
            P(),
            P(),
            P(),
            P(),
            P(),
            P(),
            P(),
            P("dp", "tm"),
            P("dp", "tm"),
            P("dp", "tm"),
        ),
        out_specs=P("dp", "tm", None),
        check_vma=False,
    )
```

```python
import functools
import jax
import jax.numpy as jnp
from jax import lax
from jax.experimental import pallas as pl
from jax.experimental.pallas import tpu as pltpu
from jax.sharding import PartitionSpec as P

MESH = pl.DeviceIdType.MESH
F32 = jnp.float32
BF16 = jnp.bfloat16
SIDE = 48
HALF = SIDE // 2
PAD = 8
STEPS = 12
LOTS = 6
LAG = 3
KEEP = 9
LEAD = 3


def silu(v):
    return v / (1.0 + jnp.exp(-v))


def span(i):
    return (0, 6) if i == 0 else (4 * i + 2, 2 if i == STEPS - 1 else 4)


def live_factors(counts, first, videos):
    def segment(moment):
        at = moment.astype(F32)
        total = jnp.zeros((1, 1), F32)
        bound = jnp.zeros((1, 1), F32)
        for i in range(videos):
            bound = bound + counts[0:1, i : i + 1]
            total = total + jnp.where(at >= bound, 1.0, 0.0)
        return total

    seg = {d: segment(first + d) for d in (-2, -1, 0, 1)}

    def live(frame, distance):
        same = jnp.where(seg[frame] == seg[frame - distance], 1.0, 0.0)
        there = jnp.where(first + frame - distance >= 0, 1.0, 0.0).astype(F32)
        return jnp.broadcast_to(same * there, (1, 128)).astype(BF16)

    return live


def body(
    rows,
    pack,
    n_tm,
    n_dp,
    videos,
    names,
    feat,
    counts_in,
    w1_in,
    b1_in,
    sw_in,
    sb_in,
    w2_in,
    b2_in,
    bucket_in,
    owner_in,
    offset_in,
    out,
    raw,
    p1,
    p2,
    w1,
    w2,
    sw,
    counts,
    b1,
    sb,
    b2,
    bucket,
    owner,
    offset,
    wm1,
    wm2,
    cnt,
    rsend,
    rrecv,
    fs,
    stage,
    psend,
    patches,
    meta,
    metas,
    hot,
    got,
    outv,
    load_sem,
    own_sem,
    out_sem,
    csend_sem,
    crecv_sem,
    xsend_sem,
    xrecv_sem,
    nsend_sem,
    nrecv_sem,
    fsend_sem,
    frecv_sem,
    rsend_sem,
    rrecv_sem,
    gsend_sem,
    grecv_sem,
    psend_sem,
    precv_sem,
    msend_sem,
    mrecv_sem,
):
    dp = lax.axis_index("dp")
    tm = lax.axis_index("tm")
    core = lax.rem(dp, 2)
    side = lax.rem(tm, 2)
    late = core == side
    early = core != side
    twin = dp + 1 - 2 * core
    across = (dp, tm + 1 - 2 * side)
    late_at = late.astype(jnp.int32)
    ahead = (twin, lax.rem(tm + 2 * late_at, n_tm))
    above = (twin, lax.rem(tm + 2, n_tm))
    below = (twin, lax.rem(tm + n_tm - 2, n_tm))
    row = dp - core + side
    slab = tm - side + late_at
    up = late & (tm < n_tm - 2)
    down = early & (tm > 1)
    lift = early & (side == 1) & (tm < n_tm - 2)
    land = down & (side == 0)
    lift_to = (twin, lax.rem(tm + 1, n_tm))
    land_from = (twin, lax.rem(tm + n_tm - 1, n_tm))
    has_next = early | up
    has_prev = late | down
    pairs = n_dp // 2
    home = dp - core + lax.rem(side + core + 1, 2)
    lot = 2 * HALF
    across_tm = jnp.where(core == 0, tm + 1 - 2 * side, tm)

    loads = [
        pltpu.make_async_copy(src, dst, load_sem.at[i])
        for i, (src, dst) in enumerate(
            (
                (counts_in, counts),
                (owner_in, owner),
                (offset_in, offset),
                (bucket_in, bucket),
                (w1_in, w1),
                (w2_in, w2),
                (sw_in, sw),
                (b1_in, b1),
                (sb_in, sb),
                (b2_in, b2),
            )
        )
    ]
    load_own = pltpu.make_async_copy(feat.at[0], raw.at[side], own_sem)

    barrier = pltpu.get_barrier_semaphore()
    for k in range(1, n_dp):
        pl.semaphore_signal(
            barrier, inc=1, device_id=(lax.rem(dp + k, n_dp), tm), device_id_type=MESH
        )

    pl.semaphore_signal(barrier, inc=1, device_id=across, device_id_type=MESH)

    @pl.when(core == 0)
    def _():
        for k in range(1, pairs):
            pl.semaphore_signal(
                barrier,
                inc=1,
                device_id=(lax.rem(dp + 2 * k, n_dp), across_tm),
                device_id_type=MESH,
            )

    @pl.when(up)
    def _():
        pl.semaphore_signal(barrier, inc=1, device_id=above, device_id_type=MESH)

    @pl.when(down)
    def _():
        pl.semaphore_signal(barrier, inc=1, device_id=below, device_id_type=MESH)

    @pl.when(lift)
    def _():
        pl.semaphore_signal(barrier, inc=1, device_id=lift_to, device_id_type=MESH)

    @pl.when(land)
    def _():
        pl.semaphore_signal(barrier, inc=1, device_id=land_from, device_id_type=MESH)

    for load in loads:
        load.start()
    links = sum(flag.astype(jnp.int32) for flag in (up, down, lift, land))
    pl.semaphore_wait(barrier, n_dp + links + (1 - core) * (pairs - 1))

    def cross_copy(y0, n, i):
        return pltpu.make_async_remote_copy(
            src_ref=feat.at[0, :, pl.ds(y0, n)],
            dst_ref=raw.at[side, :, pl.ds(y0, n)],
            send_sem=xsend_sem.at[i],
            recv_sem=xrecv_sem.at[i],
            device_id=across,
            device_id_type=MESH,
        )

    def near_copy(src, y0, n, i):
        return pltpu.make_async_remote_copy(
            src_ref=src.at[:, pl.ds(y0, n)],
            dst_ref=raw.at[1, :, pl.ds(y0, n)],
            send_sem=nsend_sem.at[i],
            recv_sem=nrecv_sem.at[i],
            device_id=(twin, tm),
            device_id_type=MESH,
        )

    def far_copy(src, y0, n, i):
        return pltpu.make_async_remote_copy(
            src_ref=src.at[:, pl.ds(y0, n)],
            dst_ref=raw.at[0, :, pl.ds(y0, n)],
            send_sem=fsend_sem.at[i],
            recv_sem=frecv_sem.at[i],
            device_id=above,
            device_id_type=MESH,
        )

    def lift_copy(y0, n, i):
        return pltpu.make_async_remote_copy(
            src_ref=feat.at[0, :, pl.ds(y0, n)],
            dst_ref=raw.at[0, :, pl.ds(y0, n)],
            send_sem=fsend_sem.at[i],
            recv_sem=frecv_sem.at[i],
            device_id=lift_to,
            device_id_type=MESH,
        )

    def count_copy():
        return pltpu.make_async_remote_copy(
            src_ref=cnt.at[0],
            dst_ref=cnt.at[1],
            send_sem=csend_sem,
            recv_sem=crecv_sem,
            device_id=(twin, tm),
            device_id_type=MESH,
        )

    def red_copy(i):
        at = pl.ds(pl.multiple_of(i * 96, 96), 96)
        return pltpu.make_async_remote_copy(
            src_ref=rsend.at[at],
            dst_ref=rrecv.at[at],
            send_sem=rsend_sem.at[i],
            recv_sem=rrecv_sem.at[i],
            device_id=ahead,
            device_id_type=MESH,
        )

    def slot_of(d):
        return pl.ds(pl.multiple_of(d * lot, lot), lot)

    def send_copy(j, k):
        return pltpu.make_async_remote_copy(
            src_ref=psend.at[j],
            dst_ref=patches.at[j, slot_of(row)],
            send_sem=psend_sem.at[j, k],
            recv_sem=precv_sem.at[j, k],
            device_id=(lax.rem(dp + 2 * k, n_dp), across_tm),
            device_id_type=MESH,
        )

    def pass_copy(j, k):
        at = slot_of(lax.rem(home + n_dp - 2 * k, n_dp))
        return pltpu.make_async_remote_copy(
            src_ref=patches.at[j, at],
            dst_ref=patches.at[j, at],
            send_sem=gsend_sem.at[j, k],
            recv_sem=grecv_sem.at[j, k],
            device_id=(twin, tm),
            device_id_type=MESH,
        )

    def meta_copy(k):
        return pltpu.make_async_remote_copy(
            src_ref=meta,
            dst_ref=metas.at[dp],
            send_sem=msend_sem.at[k],
            recv_sem=mrecv_sem.at[k],
            device_id=(lax.rem(dp + k, n_dp), tm),
            device_id_type=MESH,
        )

    @pl.when(early)
    def _():
        for i in range(STEPS):
            cross_copy(*span(i), i).start()

    @pl.when(lift)
    def _():
        for i in range(KEEP, STEPS):
            lift_copy(*span(i), i).start()

    @pl.when(late)
    def _():
        load_own.start()

        @pl.when(side == 0)
        def _():
            for i in range(STEPS):
                near_copy(feat.at[0], *span(i), i).start()

        @pl.when((side == 1) & up)
        def _():
            for i in range(LEAD):
                far_copy(feat.at[0], *span(i), i).start()

    loads[0].wait()
    cnt[0] = jnp.zeros((8, 128), F32)
    cnt[0, 0:1, 0:videos] = counts[...].astype(F32)

    @pl.when(late)
    def _():
        count_copy().start()

    for load in loads[1:4]:
        load.wait()
    code = (owner[...] * pack + offset[...] + 1).astype(F32)
    named = jnp.concatenate(
        [code, bucket[...].astype(F32), jnp.zeros((6, rows), F32)], axis=0
    )
    frame = rows // 2
    meta[...] = jnp.concatenate(
        [
            named[:, f * frame + j * HALF : f * frame + j * HALF + HALF]
            for j in range(LOTS)
            for f in range(2)
        ],
        axis=1,
    )
    metas[dp] = meta[...]
    for k in range(1, n_dp):
        meta_copy(k).start()

    for field, side_len in ((p1, SIDE), (p2, HALF)):
        wide = field.shape[2]
        for s in range(4):
            field[s, :, 0:PAD] = jnp.zeros((side_len + 2, PAD, 128), F32)
            field[s, :, PAD + side_len : wide] = jnp.zeros((side_len + 2, PAD, 128), F32)
            field[s, 0] = jnp.zeros((wide, 128), F32)
            field[s, side_len + 1] = jnp.zeros((wide, 128), F32)

    @pl.when(jnp.logical_not(has_prev))
    def _():
        p1[0:2] = jnp.zeros((2,) + p1.shape[1:], F32)
        p2[0:2] = jnp.zeros((2,) + p2.shape[1:], F32)

    @pl.when(early)
    def _():
        count_copy().wait_recv()

    @pl.when(late)
    def _():
        cnt[1] = cnt[0]

    live = live_factors(cnt[1], slab * 2, videos)
    for load in loads[4:]:
        load.wait()
    for w, wm in ((w1, wm1), (w2, wm2)):
        wm[0, :, 0:128] = w[0] * live(0, 2)
        wm[1, :, 0:128] = w[1] * live(0, 1)
        wm[1, :, 128:256] = w[0] * live(1, 2)
        wm[2, :, 0:128] = w[2]
        wm[2, :, 128:256] = w[1] * live(1, 1)

    def mm(a, w):
        return jnp.dot(a, w, preferred_element_type=F32)

    def widen(pair, y0, n):
        for f in range(2):
            p1[2 * pair + f, pl.ds(1 + y0, n), PAD : PAD + SIDE, :] = raw[
                pair, f, pl.ds(y0, n)
            ].astype(F32)

    def take(y0, n, i):
        @pl.when(late)
        def _():
            cross_copy(y0, n, i).wait_recv()

            @pl.when((side == 0) & up & (i < KEEP))
            def _():
                far_copy(raw.at[1], y0, n, i).start()

            @pl.when(side == 1)
            def _():
                near_copy(raw.at[0], y0, n, i).start()

        @pl.when(early)
        def _():
            near_copy(raw.at[1], y0, n, i).wait_recv()

        @pl.when(down)
        def _():
            far_copy(raw.at[0], y0, n, i).wait_recv()

        widen(1, y0, n)

        @pl.when(has_prev)
        def _():
            widen(0, y0, n)

    def field1(s, y0):
        sides = []
        for parity in range(2):
            parts = []
            for dy in range(3):
                for dx in range(3):
                    v = p1[s, pl.ds(y0 + dy, 4), pl.ds(PAD + parity + dx - 1, 24, stride=2), :]
                    parts.append(v.reshape(96, 128).astype(BF16))
            sides.append(jnp.concatenate(parts, axis=1))
        return jnp.concatenate(sides, axis=0)

    def field2(s, y0):
        parts = []
        for dy in range(3):
            for dx in range(3):
                v = p2[s, pl.ds(y0 + dy, 4), PAD + dx - 1 : PAD + dx + 23, :]
                parts.append(v.reshape(96, 128).astype(BF16))
        return jnp.concatenate(parts, axis=1)

    def conv(field, y0, wm, w):
        both = mm(field(1, y0), wm[1]) + mm(field(2, y0), wm[2])
        ends = (mm(field(0, y0), wm[0, :, 0:128]), mm(field(3, y0), w[2]))
        return [both[:, f * 128 : f * 128 + 128] + ends[f] for f in range(2)]

    def section_one(i):
        y0 = 4 * i
        zs = conv(field1, y0, wm1, w1)
        blocks = []
        for f in range(2):
            z = (zs[f] + b1[...]).reshape(2, 2, 2, 24, 128)
            parts = {}
            for parity in range(2):
                x = p1[2 + f, pl.ds(1 + y0, 4), pl.ds(PAD + parity, 24, stride=2), :]
                x = x.reshape(2, 2, 24, 128)
                for by in range(2):
                    parts[by, parity] = (
                        (x[:, by] + silu(z[parity, :, by])).reshape(48, 128).astype(BF16)
                    )
            blocks.append(
                jnp.concatenate(
                    [parts[by, parity] for by in range(2) for parity in range(2)], axis=1
                )
            )
        red = (mm(jnp.concatenate(blocks, axis=0), sw[...]) + sb[...]).astype(BF16)
        rsend[pl.ds(pl.multiple_of(i * 96, 96), 96), :] = red

        @pl.when(has_next)
        def _():
            red_copy(i).start()

        wide = red.astype(F32).reshape(2, 2, 24, 128)
        for f in range(2):
            p2[2 + f, pl.ds(1 + 2 * i, 2), PAD : PAD + HALF, :] = wide[f]

    def take_red(i):
        red_copy(i).wait_recv()
        wide = rrecv[pl.ds(pl.multiple_of(i * 96, 96), 96), :].astype(F32)
        wide = wide.reshape(2, 2, 24, 128)
        for f in range(2):
            p2[f, pl.ds(1 + 2 * i, 2), PAD : PAD + HALF, :] = wide[f]

    def section_two(j):
        @pl.when(has_prev)
        def _():
            @pl.when(j == 0)
            def _():
                take_red(0)

            take_red(2 * j + 1)

            @pl.when(j < LOTS - 1)
            def _():
                take_red(2 * j + 2)

        y0 = 4 * j
        zs = conv(field2, y0, wm2, w2)
        for f in range(2):
            x = p2[2 + f, pl.ds(1 + y0, 4), PAD : PAD + HALF, :].reshape(96, 128)
            fs[f] = x + silu(zs[f] + b2[...])
            for b in range(2):
                for by in range(2):
                    for bx in range(2):
                        lane = (by * 2 + bx) * 128
                        to = f * 24 + b * 12
                        stage[to : to + 12, lane : lane + 128] = fs[
                            f, pl.ds(48 * b + 24 * by + bx, 12, stride=2), :
                        ]
        done = stage[...].astype(BF16)
        psend[j] = done
        for k in range(1, pairs):
            send_copy(j, k).start()

        @pl.when(core == 0)
        def _():
            send_copy(j, 0).start()

        @pl.when(core == 1)
        def _():
            patches[j, slot_of(home), :] = done
            pass_copy(j, 0).start()

    def hand_on(j):
        @pl.when(core == 0)
        def _():
            send_copy(j, 0).wait_recv()
            pass_copy(j, 0).start()

        for k in range(1, pairs):
            send_copy(j, k).wait_recv()
            pass_copy(j, k).start()

    def prepare():
        for k in range(1, n_dp):
            meta_copy(k).wait_recv()
        slot = lax.broadcasted_iota(jnp.int32, (pack, n_dp * lot), 0) + (dp * pack + 1)
        slot = slot.astype(F32)
        at = lax.broadcasted_iota(jnp.int32, (128, n_dp * lot), 0)
        name = lax.rem(at, names).astype(F32)
        inside = at < 3 * names
        sel = jnp.zeros((pack, 128), F32)
        for j in range(LOTS):
            both = jnp.concatenate(
                [metas[d, :, j * lot : j * lot + lot] for d in range(n_dp)], axis=1
            )
            marks = jnp.where(slot == both[0:1], 1.0, 0.0).astype(BF16)
            hot[j] = marks
            chosen = jnp.where((name == both[1:2]) & inside, 1.0, 0.0).astype(BF16)
            sel = sel + lax.dot_general(
                marks, chosen, (((1,), (1,)), ((), ())), preferred_element_type=F32
            )
        outv[:, 512:640] = sel.astype(BF16)

    @pl.when(late)
    def _():
        load_own.wait()

    sink = early & (side == 0)
    pass_at = jnp.where(sink, 7, 20)
    pass_by = jnp.where(sink, 2, 1)

    def advance(s, carry):
        @pl.when(s < STEPS)
        def _():
            @pl.when(s == 0)
            def _():
                take(*span(0), 0)

            @pl.when((s > 0) & (s < STEPS - 1))
            def _():
                take(4 * s + 2, 4, s)

            @pl.when(s == STEPS - 1)
            def _():
                take(*span(STEPS - 1), STEPS - 1)

            section_one(s)

        @pl.when(late & (s == STEPS))
        def _():
            prepare()

        def turn(start, by, fn):
            t = s - start
            ready = (t >= 0) & (t < by * LOTS) & (lax.rem(t + 2 * STEPS * by, by) == 0)

            @pl.when(ready)
            def _():
                fn(t // by)

        @pl.when((side == 1) & up)
        def _():
            @pl.when(s < STEPS - 1 - LEAD)
            def _():
                far_copy(feat.at[0], 4 * (s + LEAD) + 2, 4, s + LEAD).start()

            @pl.when(s == STEPS - 1 - LEAD)
            def _():
                far_copy(feat.at[0], *span(STEPS - 1), STEPS - 1).start()

        turn(2 + 2 * LAG * late_at, 2, section_two)
        turn(pass_at, pass_by, hand_on)
        return carry

    @pl.when(early)
    def _():
        prepare()

    lax.fori_loop(0, 26, advance, 0)

    def arrive(j):
        for k in range(pairs):
            pass_copy(j, k).wait_recv()

    for j in range(LOTS - 1):
        arrive(j)
    total = mm(hot[0], patches[0])
    for j in range(1, LOTS - 1):
        total = total + mm(hot[j], patches[j])
    got[...] = total
    arrive(LOTS - 1)
    tile = pack // 2
    stores = []
    for m in range(2):
        at = pl.ds(m * tile, tile)
        rest = got[at] + mm(hot[LOTS - 1, at], patches[LOTS - 1])
        outv[at, 0:512] = rest.astype(BF16)
        stores.append(pltpu.make_async_copy(outv.at[at], out.at[at], out_sem.at[m]))
        stores[m].start()

    @pl.when(early)
    def _():
        for i in range(STEPS):
            cross_copy(*span(i), i).wait_send()

    @pl.when(late)
    def _():
        count_copy().wait_send()
        for i in range(STEPS):
            near_copy(raw.at[0], *span(i), i).wait_send()

    @pl.when(up)
    def _():
        for i in range(KEEP):
            far_copy(raw.at[1], *span(i), i).wait_send()

    @pl.when((up & (side == 1)) | lift)
    def _():
        for i in range(KEEP, STEPS):
            far_copy(raw.at[1], *span(i), i).wait_send()

    @pl.when(core == 0)
    def _():
        for j in range(LOTS):
            send_copy(j, 0).wait_send()

    @pl.when(has_next)
    def _():
        for i in range(STEPS):
            red_copy(i).wait_send()

    for k in range(1, n_dp):
        meta_copy(k).wait_send()
    for j in range(LOTS):
        for k in range(1, pairs):
            send_copy(j, k).wait_send()
        for k in range(pairs):
            pass_copy(j, k).wait_send()
    for store in stores:
        store.wait()


def embed(packed, ew, eb, table, out):
    names = table.shape[0]
    full = table[...] + eb[...].reshape(1, -1)
    high = full.astype(BF16).astype(F32)
    mid = (full - high).astype(BF16).astype(F32)
    low = full - high - mid
    split = jnp.concatenate(
        [high, mid, low, jnp.zeros((128 - 3 * names, full.shape[1]), F32)], axis=0
    ).astype(BF16)
    total = jnp.dot(packed[:, 0:512], ew[...], preferred_element_type=F32)
    total = total + jnp.dot(packed[:, 512:640], split, preferred_element_type=F32)
    out[...] = total.astype(BF16)


def shards(
    n_dp,
    n_tm,
    features,
    frame_counts,
    conv1_weight,
    conv1_bias,
    shrink_weight,
    shrink_bias,
    conv2_weight,
    conv2_bias,
    embed_weight,
    embed_bias,
    bucket_table,
    bucket_ids,
    dest_owner,
    dest_offset,
):
    rows = dest_owner.shape[1]
    pack = 2 * rows
    lat = embed_weight.shape[1]
    videos = frame_counts.shape[1]
    anywhere = pl.BlockSpec(memory_space=pl.ANY)
    pairs = n_dp // 2
    lot = 2 * HALF
    dma = pltpu.SemaphoreType.DMA
    gathered = pl.pallas_call(
        functools.partial(body, rows, pack, n_tm, n_dp, videos, bucket_table.shape[0]),
        out_shape=pltpu.VMEM((pack, 640), BF16),
        in_specs=[anywhere] * 11,
        out_specs=anywhere,
        scratch_shapes=[
            pltpu.VMEM((2, 2, SIDE, SIDE, 128), BF16),
            pltpu.VMEM((4, SIDE + 2, SIDE + 2 * PAD, 128), F32),
            pltpu.VMEM((4, HALF + 2, HALF + 2 * PAD, 128), F32),
            pltpu.VMEM((3, 1152, 128), BF16),
            pltpu.VMEM((3, 1152, 128), BF16),
            pltpu.VMEM((512, 128), BF16),
            pltpu.VMEM((1, videos), jnp.int32),
            pltpu.VMEM((1, 128), F32),
            pltpu.VMEM((1, 128), F32),
            pltpu.VMEM((1, 128), F32),
            pltpu.VMEM((1, rows), jnp.int32),
            pltpu.VMEM((1, rows), jnp.int32),
            pltpu.VMEM((1, rows), jnp.int32),
            pltpu.VMEM((3, 1152, 256), BF16),
            pltpu.VMEM((3, 1152, 256), BF16),
            pltpu.VMEM((2, 8, 128), F32),
            pltpu.VMEM((STEPS * 96, 128), BF16),
            pltpu.VMEM((STEPS * 96, 128), BF16),
            pltpu.VMEM((2, 96, 128), F32),
            pltpu.VMEM((lot, 512), F32),
            pltpu.VMEM((LOTS, lot, 512), BF16),
            pltpu.VMEM((LOTS, n_dp * lot, 512), BF16),
            pltpu.VMEM((8, rows), F32),
            pltpu.VMEM((n_dp, 8, rows), F32),
            pltpu.VMEM((LOTS, pack, n_dp * lot), BF16),
            pltpu.VMEM((pack, 512), F32),
            pltpu.VMEM((pack, 640), BF16),
            dma((10,)),
            dma,
            dma((2,)),
            dma,
            dma,
            dma((STEPS,)),
            dma((STEPS,)),
            dma((STEPS,)),
            dma((STEPS,)),
            dma((STEPS,)),
            dma((STEPS,)),
            dma((STEPS,)),
            dma((STEPS,)),
            dma((LOTS, pairs)),
            dma((LOTS, pairs)),
            dma((LOTS, pairs)),
            dma((LOTS, pairs)),
            dma((n_dp,)),
            dma((n_dp,)),
        ],
        compiler_params=pltpu.CompilerParams(
            collective_id=0, has_side_effects=True, vmem_limit_bytes=56 * 1024 * 1024
        ),
        name="encoder",
    )(
        features,
        frame_counts,
        conv1_weight.reshape(3, 1152, 128),
        conv1_bias.reshape(1, 128),
        shrink_weight,
        shrink_bias.reshape(1, 128),
        conv2_weight.reshape(3, 1152, 128),
        conv2_bias.reshape(1, 128),
        bucket_ids,
        dest_owner,
        dest_offset,
    )
    tile = pack // 2
    packed = pl.pallas_call(
        embed,
        grid=(2,),
        out_shape=jax.ShapeDtypeStruct((pack, lat), BF16),
        in_specs=[
            pl.BlockSpec((tile, 640), lambda i: (i, 0)),
            pl.BlockSpec((512, lat), lambda i: (0, 0)),
            pl.BlockSpec((lat,), lambda i: (0,)),
            pl.BlockSpec(bucket_table.shape, lambda i: (0, 0)),
        ],
        out_specs=pl.BlockSpec((tile, lat), lambda i: (i, 0)),
        compiler_params=pltpu.CompilerParams(vmem_limit_bytes=48 * 1024 * 1024),
        name="embed",
    )(gathered, embed_weight, embed_bias, bucket_table)
    return packed[None]


def solution(mesh):
    sizes = dict(mesh.shape)
    return jax.shard_map(
        functools.partial(shards, sizes["dp"], sizes["tm"]),
        mesh=mesh,
        in_specs=(
            P("dp", "tm", None, None, None),
            P("dp", None),
            P(),
            P(),
            P(),
            P(),
            P(),
            P(),
            P(),
            P(),
            P(),
            P("dp", "tm"),
            P("dp", "tm"),
            P("dp", "tm"),
        ),
        out_specs=P("dp", "tm", None),
        check_vma=False,
    )
```

```python
import functools
import jax
import jax.numpy as jnp
from jax import lax
from jax.experimental import pallas as pl
from jax.experimental.pallas import tpu as pltpu
from jax.sharding import PartitionSpec as P

MESH = pl.DeviceIdType.MESH
F32 = jnp.float32
BF16 = jnp.bfloat16
SIDE = 48
HALF = SIDE // 2
PAD = 8
STEPS = 12
PIECES = STEPS + 1
LOTS = 6
LAG = 3
LEAD = 3
TILES = 4


def silu(v):
    return v / (1.0 + jnp.exp(-v))


def span(i):
    return (0, 2) if i == 0 else (4 * i - 2, 2 if i == STEPS else 4)


def live_factors(counts, first, videos):
    def segment(moment):
        at = moment.astype(F32)
        total = jnp.zeros((1, 1), F32)
        bound = jnp.zeros((1, 1), F32)
        for i in range(videos):
            bound = bound + counts[0:1, i : i + 1]
            total = total + jnp.where(at >= bound, 1.0, 0.0)
        return total

    seg = {d: segment(first + d) for d in (-2, -1, 0, 1)}

    def live(frame, distance):
        same = jnp.where(seg[frame] == seg[frame - distance], 1.0, 0.0)
        there = jnp.where(first + frame - distance >= 0, 1.0, 0.0).astype(F32)
        return jnp.broadcast_to(same * there, (1, 128)).astype(BF16)

    return live


def body(
    rows,
    pack,
    n_tm,
    n_dp,
    videos,
    names,
    feat,
    counts_in,
    w1_in,
    b1_in,
    sw_in,
    sb_in,
    w2_in,
    b2_in,
    bucket_in,
    owner_in,
    offset_in,
    out,
    raw,
    p1,
    p2,
    w1,
    w2,
    sw,
    counts,
    b1,
    sb,
    b2,
    bucket,
    owner,
    offset,
    wm1,
    wm2,
    cnt,
    rsend,
    rrecv,
    fs,
    stage,
    psend,
    patches,
    meta,
    metas,
    hot,
    got,
    outv,
    load_sem,
    own_sem,
    out_sem,
    csend_sem,
    crecv_sem,
    xsend_sem,
    xrecv_sem,
    nsend_sem,
    nrecv_sem,
    fsend_sem,
    frecv_sem,
    rsend_sem,
    rrecv_sem,
    gsend_sem,
    grecv_sem,
    psend_sem,
    precv_sem,
    msend_sem,
    mrecv_sem,
):
    dp = lax.axis_index("dp")
    tm = lax.axis_index("tm")
    core = lax.rem(dp, 2)
    side = lax.rem(tm, 2)
    late = core == side
    early = core != side
    twin = dp + 1 - 2 * core
    across = (dp, tm + 1 - 2 * side)
    late_at = late.astype(jnp.int32)
    ahead = (twin, lax.rem(tm + 2 * late_at, n_tm))
    above = (twin, lax.rem(tm + 2, n_tm))
    below = (twin, lax.rem(tm + n_tm - 2, n_tm))
    row = dp - core + side
    slab = tm - side + late_at
    up = late & (tm < n_tm - 2)
    down = early & (tm > 1)
    has_next = early | up
    has_prev = late | down
    pairs = n_dp // 2
    home = dp - core + lax.rem(side + core + 1, 2)
    lot = 2 * HALF
    across_tm = jnp.where(core == 0, tm + 1 - 2 * side, tm)

    loads = [
        pltpu.make_async_copy(src, dst, load_sem.at[i])
        for i, (src, dst) in enumerate(
            (
                (counts_in, counts),
                (owner_in, owner),
                (offset_in, offset),
                (bucket_in, bucket),
                (w1_in, w1),
                (w2_in, w2),
                (sw_in, sw),
                (b1_in, b1),
                (sb_in, sb),
                (b2_in, b2),
            )
        )
    ]
    load_own = pltpu.make_async_copy(feat.at[0], raw.at[side], own_sem)

    barrier = pltpu.get_barrier_semaphore()
    for k in range(1, n_dp):
        pl.semaphore_signal(
            barrier, inc=1, device_id=(lax.rem(dp + k, n_dp), tm), device_id_type=MESH
        )

    pl.semaphore_signal(barrier, inc=1, device_id=across, device_id_type=MESH)

    @pl.when(core == 0)
    def _():
        for k in range(1, pairs):
            pl.semaphore_signal(
                barrier,
                inc=1,
                device_id=(lax.rem(dp + 2 * k, n_dp), across_tm),
                device_id_type=MESH,
            )

    @pl.when(up)
    def _():
        pl.semaphore_signal(barrier, inc=1, device_id=above, device_id_type=MESH)

    @pl.when(down)
    def _():
        pl.semaphore_signal(barrier, inc=1, device_id=below, device_id_type=MESH)

    for load in loads:
        load.start()
    links = up.astype(jnp.int32) + down.astype(jnp.int32)
    pl.semaphore_wait(barrier, n_dp + links + (1 - core) * (pairs - 1))

    def cross_copy(y0, n, i):
        return pltpu.make_async_remote_copy(
            src_ref=feat.at[0, :, pl.ds(y0, n)],
            dst_ref=raw.at[side, :, pl.ds(y0, n)],
            send_sem=xsend_sem.at[i],
            recv_sem=xrecv_sem.at[i],
            device_id=across,
            device_id_type=MESH,
        )

    def near_copy(src, y0, n, i):
        return pltpu.make_async_remote_copy(
            src_ref=src.at[:, pl.ds(y0, n)],
            dst_ref=raw.at[1, :, pl.ds(y0, n)],
            send_sem=nsend_sem.at[i],
            recv_sem=nrecv_sem.at[i],
            device_id=(twin, tm),
            device_id_type=MESH,
        )

    def far_copy(src, y0, n, i):
        return pltpu.make_async_remote_copy(
            src_ref=src.at[:, pl.ds(y0, n)],
            dst_ref=raw.at[0, :, pl.ds(y0, n)],
            send_sem=fsend_sem.at[i],
            recv_sem=frecv_sem.at[i],
            device_id=above,
            device_id_type=MESH,
        )

    def count_copy():
        return pltpu.make_async_remote_copy(
            src_ref=cnt.at[0],
            dst_ref=cnt.at[1],
            send_sem=csend_sem,
            recv_sem=crecv_sem,
            device_id=(twin, tm),
            device_id_type=MESH,
        )

    def red_copy(i):
        at = pl.ds(pl.multiple_of(i * 96, 96), 96)
        return pltpu.make_async_remote_copy(
            src_ref=rsend.at[at],
            dst_ref=rrecv.at[at],
            send_sem=rsend_sem.at[i],
            recv_sem=rrecv_sem.at[i],
            device_id=ahead,
            device_id_type=MESH,
        )

    def slot_of(d):
        return pl.ds(pl.multiple_of(d * lot, lot), lot)

    def send_copy(j, k):
        return pltpu.make_async_remote_copy(
            src_ref=psend.at[j],
            dst_ref=patches.at[j, slot_of(row)],
            send_sem=psend_sem.at[j, k],
            recv_sem=precv_sem.at[j, k],
            device_id=(lax.rem(dp + 2 * k, n_dp), across_tm),
            device_id_type=MESH,
        )

    def pass_copy(j, k):
        at = slot_of(lax.rem(home + n_dp - 2 * k, n_dp))
        return pltpu.make_async_remote_copy(
            src_ref=patches.at[j, at],
            dst_ref=patches.at[j, at],
            send_sem=gsend_sem.at[j, k],
            recv_sem=grecv_sem.at[j, k],
            device_id=(twin, tm),
            device_id_type=MESH,
        )

    def meta_copy(k):
        return pltpu.make_async_remote_copy(
            src_ref=meta,
            dst_ref=metas.at[dp],
            send_sem=msend_sem.at[k],
            recv_sem=mrecv_sem.at[k],
            device_id=(lax.rem(dp + k, n_dp), tm),
            device_id_type=MESH,
        )

    @pl.when(early)
    def _():
        for i in range(PIECES):
            cross_copy(*span(i), i).start()

    @pl.when(late)
    def _():
        load_own.start()

        @pl.when(side == 0)
        def _():
            for i in range(PIECES):
                near_copy(feat.at[0], *span(i), i).start()

        @pl.when((side == 1) & up)
        def _():
            for i in range(LEAD):
                far_copy(feat.at[0], *span(i), i).start()

    loads[0].wait()
    cnt[0] = jnp.zeros((8, 128), F32)
    cnt[0, 0:1, 0:videos] = counts[...].astype(F32)

    @pl.when(late)
    def _():
        count_copy().start()

    for load in loads[1:4]:
        load.wait()
    code = (owner[...] * pack + offset[...] + 1).astype(F32)
    named = jnp.concatenate(
        [code, bucket[...].astype(F32), jnp.zeros((6, rows), F32)], axis=0
    )
    frame = rows // 2
    meta[...] = jnp.concatenate(
        [
            named[:, f * frame + j * HALF : f * frame + j * HALF + HALF]
            for j in range(LOTS)
            for f in range(2)
        ],
        axis=1,
    )
    metas[dp] = meta[...]
    for k in range(1, n_dp):
        meta_copy(k).start()

    for field, side_len in ((p1, SIDE), (p2, HALF)):
        wide = field.shape[2]
        for s in range(4):
            field[s, :, 0:PAD] = jnp.zeros((side_len + 2, PAD, 128), F32)
            field[s, :, PAD + side_len : wide] = jnp.zeros((side_len + 2, PAD, 128), F32)
            field[s, 0] = jnp.zeros((wide, 128), F32)
            field[s, side_len + 1] = jnp.zeros((wide, 128), F32)

    @pl.when(jnp.logical_not(has_prev))
    def _():
        p1[0:2] = jnp.zeros((2,) + p1.shape[1:], F32)
        p2[0:2] = jnp.zeros((2,) + p2.shape[1:], F32)

    @pl.when(early)
    def _():
        count_copy().wait_recv()

    @pl.when(late)
    def _():
        cnt[1] = cnt[0]

    live = live_factors(cnt[1], slab * 2, videos)
    for load in loads[4:]:
        load.wait()
    for w, wm in ((w1, wm1), (w2, wm2)):
        wm[0, :, 0:128] = w[0] * live(0, 2)
        wm[1, :, 0:128] = w[1] * live(0, 1)
        wm[1, :, 128:256] = w[0] * live(1, 2)
        wm[2, :, 0:128] = w[2]
        wm[2, :, 128:256] = w[1] * live(1, 1)

    def mm(a, w):
        return jnp.dot(a, w, preferred_element_type=F32)

    def widen(pair, y0, n):
        for f in range(2):
            p1[2 * pair + f, pl.ds(1 + y0, n), PAD : PAD + SIDE, :] = raw[
                pair, f, pl.ds(y0, n)
            ].astype(F32)

    def take(y0, n, i):
        @pl.when(late)
        def _():
            cross_copy(y0, n, i).wait_recv()

            @pl.when((side == 0) & up)
            def _():
                far_copy(raw.at[1], y0, n, i).start()

            @pl.when(side == 1)
            def _():
                near_copy(raw.at[0], y0, n, i).start()

        @pl.when(early)
        def _():
            near_copy(raw.at[1], y0, n, i).wait_recv()

        @pl.when(down)
        def _():
            far_copy(raw.at[0], y0, n, i).wait_recv()

        widen(1, y0, n)

        @pl.when(has_prev)
        def _():
            widen(0, y0, n)

    def field1(s, y0):
        sides = []
        for parity in range(2):
            parts = []
            for dy in range(3):
                for dx in range(3):
                    v = p1[s, pl.ds(y0 + dy, 4), pl.ds(PAD + parity + dx - 1, 24, stride=2), :]
                    parts.append(v.reshape(96, 128).astype(BF16))
            sides.append(jnp.concatenate(parts, axis=1))
        return jnp.concatenate(sides, axis=0)

    def field2(s, y0):
        parts = []
        for dy in range(3):
            for dx in range(3):
                v = p2[s, pl.ds(y0 + dy, 4), PAD + dx - 1 : PAD + dx + 23, :]
                parts.append(v.reshape(96, 128).astype(BF16))
        return jnp.concatenate(parts, axis=1)

    def conv(field, y0, wm, w):
        both = mm(field(1, y0), wm[1]) + mm(field(2, y0), wm[2])
        ends = (mm(field(0, y0), wm[0, :, 0:128]), mm(field(3, y0), w[2]))
        return [both[:, f * 128 : f * 128 + 128] + ends[f] for f in range(2)]

    def section_one(i):
        y0 = 4 * i
        zs = conv(field1, y0, wm1, w1)
        blocks = []
        for f in range(2):
            z = (zs[f] + b1[...]).reshape(2, 2, 2, 24, 128)
            parts = {}
            for parity in range(2):
                x = p1[2 + f, pl.ds(1 + y0, 4), pl.ds(PAD + parity, 24, stride=2), :]
                x = x.reshape(2, 2, 24, 128)
                for by in range(2):
                    parts[by, parity] = (
                        (x[:, by] + silu(z[parity, :, by])).reshape(48, 128).astype(BF16)
                    )
            blocks.append(
                jnp.concatenate(
                    [parts[by, parity] for by in range(2) for parity in range(2)], axis=1
                )
            )
        red = (mm(jnp.concatenate(blocks, axis=0), sw[...]) + sb[...]).astype(BF16)
        rsend[pl.ds(pl.multiple_of(i * 96, 96), 96), :] = red

        @pl.when(has_next)
        def _():
            red_copy(i).start()

        wide = red.astype(F32).reshape(2, 2, 24, 128)
        for f in range(2):
            p2[2 + f, pl.ds(1 + 2 * i, 2), PAD : PAD + HALF, :] = wide[f]

    def take_red(i):
        red_copy(i).wait_recv()
        wide = rrecv[pl.ds(pl.multiple_of(i * 96, 96), 96), :].astype(F32)
        wide = wide.reshape(2, 2, 24, 128)
        for f in range(2):
            p2[f, pl.ds(1 + 2 * i, 2), PAD : PAD + HALF, :] = wide[f]

    def section_two(j):
        @pl.when(has_prev)
        def _():
            @pl.when(j == 0)
            def _():
                take_red(0)

            take_red(2 * j + 1)

            @pl.when(j < LOTS - 1)
            def _():
                take_red(2 * j + 2)

        y0 = 4 * j
        zs = conv(field2, y0, wm2, w2)
        for f in range(2):
            x = p2[2 + f, pl.ds(1 + y0, 4), PAD : PAD + HALF, :].reshape(96, 128)
            fs[f] = x + silu(zs[f] + b2[...])
            for b in range(2):
                for by in range(2):
                    for bx in range(2):
                        lane = (by * 2 + bx) * 128
                        to = f * 24 + b * 12
                        stage[to : to + 12, lane : lane + 128] = fs[
                            f, pl.ds(48 * b + 24 * by + bx, 12, stride=2), :
                        ]
        done = stage[...].astype(BF16)
        psend[j] = done
        for k in range(1, pairs):
            send_copy(j, k).start()

        @pl.when(core == 0)
        def _():
            send_copy(j, 0).start()

        @pl.when(core == 1)
        def _():
            patches[j, slot_of(home), :] = done
            pass_copy(j, 0).start()

    def hand_on(j):
        @pl.when(core == 0)
        def _():
            send_copy(j, 0).wait_recv()
            pass_copy(j, 0).start()

        for k in range(1, pairs):
            send_copy(j, k).wait_recv()
            pass_copy(j, k).start()

    def prepare():
        for k in range(1, n_dp):
            meta_copy(k).wait_recv()
        slot = lax.broadcasted_iota(jnp.int32, (pack, n_dp * lot), 0) + (dp * pack + 1)
        slot = slot.astype(F32)
        at = lax.broadcasted_iota(jnp.int32, (128, n_dp * lot), 0)
        name = lax.rem(at, names).astype(F32)
        inside = at < 3 * names
        sel = jnp.zeros((pack, 128), F32)
        for j in range(LOTS):
            both = jnp.concatenate(
                [metas[d, :, j * lot : j * lot + lot] for d in range(n_dp)], axis=1
            )
            marks = jnp.where(slot == both[0:1], 1.0, 0.0).astype(BF16)
            hot[j] = marks
            chosen = jnp.where((name == both[1:2]) & inside, 1.0, 0.0).astype(BF16)
            sel = sel + lax.dot_general(
                marks, chosen, (((1,), (1,)), ((), ())), preferred_element_type=F32
            )
        outv[:, 512:640] = sel.astype(BF16)

    @pl.when(late)
    def _():
        load_own.wait()

    sink = early & (side == 0)
    pass_at = jnp.where(sink, 7, 20)
    pass_by = jnp.where(sink, 2, 1)

    def advance(s, carry):
        @pl.when(s < STEPS)
        def _():
            @pl.when(s == 0)
            def _():
                take(*span(0), 0)

            @pl.when(s < STEPS - 1)
            def _():
                take(4 * s + 2, 4, s + 1)

            @pl.when(s == STEPS - 1)
            def _():
                take(*span(STEPS), STEPS)

            section_one(s)

        @pl.when(late & (s == STEPS))
        def _():
            prepare()

        def turn(start, by, fn):
            t = s - start
            ready = (t >= 0) & (t < by * LOTS) & (lax.rem(t + 2 * STEPS * by, by) == 0)

            @pl.when(ready)
            def _():
                fn(t // by)

        @pl.when((side == 1) & up)
        def _():
            @pl.when(s < STEPS - LEAD)
            def _():
                far_copy(feat.at[0], 4 * (s + LEAD) - 2, 4, s + LEAD).start()

            @pl.when(s == STEPS - LEAD)
            def _():
                far_copy(feat.at[0], *span(STEPS), STEPS).start()

        turn(2 + 2 * LAG * late_at, 2, section_two)
        turn(pass_at, pass_by, hand_on)
        return carry

    @pl.when(early)
    def _():
        prepare()

    lax.fori_loop(0, 26, advance, 0)

    def arrive(j):
        for k in range(pairs):
            pass_copy(j, k).wait_recv()

    for j in range(LOTS - 1):
        arrive(j)
    total = mm(hot[0], patches[0])
    for j in range(1, LOTS - 1):
        total = total + mm(hot[j], patches[j])
    got[...] = total
    arrive(LOTS - 1)
    tile = pack // 2
    stores = []
    for m in range(2):
        at = pl.ds(m * tile, tile)
        rest = got[at] + mm(hot[LOTS - 1, at], patches[LOTS - 1])
        outv[at, 0:512] = rest.astype(BF16)
        stores.append(pltpu.make_async_copy(outv.at[at], out.at[at], out_sem.at[m]))
        stores[m].start()

    @pl.when(early)
    def _():
        for i in range(PIECES):
            cross_copy(*span(i), i).wait_send()

    @pl.when(late)
    def _():
        count_copy().wait_send()
        for i in range(PIECES):
            near_copy(raw.at[0], *span(i), i).wait_send()

    @pl.when(up)
    def _():
        for i in range(PIECES):
            far_copy(raw.at[1], *span(i), i).wait_send()

    @pl.when(core == 0)
    def _():
        for j in range(LOTS):
            send_copy(j, 0).wait_send()

    @pl.when(has_next)
    def _():
        for i in range(STEPS):
            red_copy(i).wait_send()

    for k in range(1, n_dp):
        meta_copy(k).wait_send()
    for j in range(LOTS):
        for k in range(1, pairs):
            send_copy(j, k).wait_send()
        for k in range(pairs):
            pass_copy(j, k).wait_send()
    for store in stores:
        store.wait()


def embed(packed, ew, eb, table, out, rows, out_sem):
    names = table.shape[0]
    full = table[...] + eb[...].reshape(1, -1)
    high = full.astype(BF16).astype(F32)
    mid = (full - high).astype(BF16).astype(F32)
    low = full - high - mid
    split = jnp.concatenate(
        [high, mid, low, jnp.zeros((128 - 3 * names, full.shape[1]), F32)], axis=0
    ).astype(BF16)
    tile = packed.shape[0] // TILES
    stores = []
    for m in range(TILES):
        at = pl.ds(m * tile, tile)
        total = jnp.dot(packed[at, 0:512], ew[...], preferred_element_type=F32)
        total = total + jnp.dot(packed[at, 512:640], split, preferred_element_type=F32)
        rows[at] = total.astype(BF16)
        stores.append(pltpu.make_async_copy(rows.at[at], out.at[at], out_sem.at[m]))
        stores[m].start()
    for store in stores:
        store.wait()


def shards(
    n_dp,
    n_tm,
    features,
    frame_counts,
    conv1_weight,
    conv1_bias,
    shrink_weight,
    shrink_bias,
    conv2_weight,
    conv2_bias,
    embed_weight,
    embed_bias,
    bucket_table,
    bucket_ids,
    dest_owner,
    dest_offset,
):
    rows = dest_owner.shape[1]
    pack = 2 * rows
    lat = embed_weight.shape[1]
    videos = frame_counts.shape[1]
    anywhere = pl.BlockSpec(memory_space=pl.ANY)
    pairs = n_dp // 2
    lot = 2 * HALF
    dma = pltpu.SemaphoreType.DMA
    gathered = pl.pallas_call(
        functools.partial(body, rows, pack, n_tm, n_dp, videos, bucket_table.shape[0]),
        out_shape=pltpu.VMEM((pack, 640), BF16),
        in_specs=[anywhere] * 11,
        out_specs=anywhere,
        scratch_shapes=[
            pltpu.VMEM((2, 2, SIDE, SIDE, 128), BF16),
            pltpu.VMEM((4, SIDE + 2, SIDE + 2 * PAD, 128), F32),
            pltpu.VMEM((4, HALF + 2, HALF + 2 * PAD, 128), F32),
            pltpu.VMEM((3, 1152, 128), BF16),
            pltpu.VMEM((3, 1152, 128), BF16),
            pltpu.VMEM((512, 128), BF16),
            pltpu.VMEM((1, videos), jnp.int32),
            pltpu.VMEM((1, 128), F32),
            pltpu.VMEM((1, 128), F32),
            pltpu.VMEM((1, 128), F32),
            pltpu.VMEM((1, rows), jnp.int32),
            pltpu.VMEM((1, rows), jnp.int32),
            pltpu.VMEM((1, rows), jnp.int32),
            pltpu.VMEM((3, 1152, 256), BF16),
            pltpu.VMEM((3, 1152, 256), BF16),
            pltpu.VMEM((2, 8, 128), F32),
            pltpu.VMEM((STEPS * 96, 128), BF16),
            pltpu.VMEM((STEPS * 96, 128), BF16),
            pltpu.VMEM((2, 96, 128), F32),
            pltpu.VMEM((lot, 512), F32),
            pltpu.VMEM((LOTS, lot, 512), BF16),
            pltpu.VMEM((LOTS, n_dp * lot, 512), BF16),
            pltpu.VMEM((8, rows), F32),
            pltpu.VMEM((n_dp, 8, rows), F32),
            pltpu.VMEM((LOTS, pack, n_dp * lot), BF16),
            pltpu.VMEM((pack, 512), F32),
            pltpu.VMEM((pack, 640), BF16),
            dma((10,)),
            dma,
            dma((2,)),
            dma,
            dma,
            dma((PIECES,)),
            dma((PIECES,)),
            dma((PIECES,)),
            dma((PIECES,)),
            dma((PIECES,)),
            dma((PIECES,)),
            dma((STEPS,)),
            dma((STEPS,)),
            dma((LOTS, pairs)),
            dma((LOTS, pairs)),
            dma((LOTS, pairs)),
            dma((LOTS, pairs)),
            dma((n_dp,)),
            dma((n_dp,)),
        ],
        compiler_params=pltpu.CompilerParams(
            collective_id=0, has_side_effects=True, vmem_limit_bytes=56 * 1024 * 1024
        ),
        name="encoder",
    )(
        features,
        frame_counts,
        conv1_weight.reshape(3, 1152, 128),
        conv1_bias.reshape(1, 128),
        shrink_weight,
        shrink_bias.reshape(1, 128),
        conv2_weight.reshape(3, 1152, 128),
        conv2_bias.reshape(1, 128),
        bucket_ids,
        dest_owner,
        dest_offset,
    )
    packed = pl.pallas_call(
        embed,
        out_shape=jax.ShapeDtypeStruct((pack, lat), BF16),
        in_specs=[pl.BlockSpec(memory_space=pltpu.VMEM)] * 4,
        out_specs=anywhere,
        scratch_shapes=[pltpu.VMEM((pack, lat), BF16), dma((TILES,))],
        compiler_params=pltpu.CompilerParams(vmem_limit_bytes=48 * 1024 * 1024),
        name="embed",
    )(gathered, embed_weight, embed_bias, bucket_table)
    return packed[None]


def solution(mesh):
    sizes = dict(mesh.shape)
    return jax.shard_map(
        functools.partial(shards, sizes["dp"], sizes["tm"]),
        mesh=mesh,
        in_specs=(
            P("dp", "tm", None, None, None),
            P("dp", None),
            P(),
            P(),
            P(),
            P(),
            P(),
            P(),
            P(),
            P(),
            P(),
            P("dp", "tm"),
            P("dp", "tm"),
            P("dp", "tm"),
        ),
        out_specs=P("dp", "tm", None),
        check_vma=False,
    )
```

```python
import functools
import jax
import jax.numpy as jnp
from jax import lax
from jax.experimental import pallas as pl
from jax.experimental.pallas import tpu as pltpu
from jax.sharding import PartitionSpec as P

MESH = pl.DeviceIdType.MESH
F32 = jnp.float32
BF16 = jnp.bfloat16
SIDE = 48
HALF = SIDE // 2
PAD = 8
STEPS = 12
PIECES = STEPS + 1
LOTS = 6
LAG = 3
LEAD = 3
TILES = 4


def silu(v):
    return v / (1.0 + jnp.exp(-v))


def span(i):
    return (0, 2) if i == 0 else (4 * i - 2, 2 if i == STEPS else 4)


def live_factors(counts, first, videos):
    def segment(moment):
        at = moment.astype(F32)
        total = jnp.zeros((1, 1), F32)
        bound = jnp.zeros((1, 1), F32)
        for i in range(videos):
            bound = bound + counts[0:1, i : i + 1]
            total = total + jnp.where(at >= bound, 1.0, 0.0)
        return total

    seg = {d: segment(first + d) for d in (-2, -1, 0, 1)}

    def live(frame, distance):
        same = jnp.where(seg[frame] == seg[frame - distance], 1.0, 0.0)
        there = jnp.where(first + frame - distance >= 0, 1.0, 0.0).astype(F32)
        return jnp.broadcast_to(same * there, (1, 128)).astype(BF16)

    return live


def body(
    rows,
    pack,
    n_tm,
    n_dp,
    videos,
    names,
    feat,
    counts_in,
    w1_in,
    b1_in,
    sw_in,
    sb_in,
    w2_in,
    b2_in,
    bucket_in,
    owner_in,
    offset_in,
    out,
    raw,
    p1,
    p2,
    w1,
    w2,
    sw,
    counts,
    b1,
    sb,
    b2,
    bucket,
    owner,
    offset,
    wm1,
    wm2,
    cnt,
    rsend,
    rrecv,
    fs,
    stage,
    psend,
    patches,
    meta,
    metas,
    hot,
    got,
    outv,
    load_sem,
    own_sem,
    out_sem,
    csend_sem,
    crecv_sem,
    xsend_sem,
    xrecv_sem,
    nsend_sem,
    nrecv_sem,
    fsend_sem,
    frecv_sem,
    rsend_sem,
    rrecv_sem,
    gsend_sem,
    grecv_sem,
    psend_sem,
    precv_sem,
    msend_sem,
    mrecv_sem,
):
    dp = lax.axis_index("dp")
    tm = lax.axis_index("tm")
    core = lax.rem(dp, 2)
    side = lax.rem(tm, 2)
    late = core == side
    early = core != side
    twin = dp + 1 - 2 * core
    across = (dp, tm + 1 - 2 * side)
    late_at = late.astype(jnp.int32)
    ahead = (twin, lax.rem(tm + 2 * late_at, n_tm))
    above = (twin, lax.rem(tm + 2, n_tm))
    below = (twin, lax.rem(tm + n_tm - 2, n_tm))
    row = dp - core + side
    slab = tm - side + late_at
    up = late & (tm < n_tm - 2)
    down = early & (tm > 1)
    has_next = early | up
    has_prev = late | down
    pairs = n_dp // 2
    home = dp - core + lax.rem(side + core + 1, 2)
    lot = 2 * HALF
    across_tm = jnp.where(core == 0, tm + 1 - 2 * side, tm)

    loads = [
        pltpu.make_async_copy(src, dst, load_sem.at[i])
        for i, (src, dst) in enumerate(
            (
                (counts_in, counts),
                (owner_in, owner),
                (offset_in, offset),
                (bucket_in, bucket),
                (w1_in, w1),
                (w2_in, w2),
                (sw_in, sw),
                (b1_in, b1),
                (sb_in, sb),
                (b2_in, b2),
            )
        )
    ]
    load_own = pltpu.make_async_copy(feat.at[0], raw.at[side], own_sem)

    barrier = pltpu.get_barrier_semaphore()
    for k in range(1, n_dp):
        pl.semaphore_signal(
            barrier, inc=1, device_id=(lax.rem(dp + k, n_dp), tm), device_id_type=MESH
        )

    pl.semaphore_signal(barrier, inc=1, device_id=across, device_id_type=MESH)

    @pl.when(core == 0)
    def _():
        for k in range(1, pairs):
            pl.semaphore_signal(
                barrier,
                inc=1,
                device_id=(lax.rem(dp + 2 * k, n_dp), across_tm),
                device_id_type=MESH,
            )

    @pl.when(up)
    def _():
        pl.semaphore_signal(barrier, inc=1, device_id=above, device_id_type=MESH)

    @pl.when(down)
    def _():
        pl.semaphore_signal(barrier, inc=1, device_id=below, device_id_type=MESH)

    for load in loads:
        load.start()
    links = up.astype(jnp.int32) + down.astype(jnp.int32)
    pl.semaphore_wait(barrier, n_dp + links + (1 - core) * (pairs - 1))

    def cross_copy(y0, n, i):
        return pltpu.make_async_remote_copy(
            src_ref=feat.at[0, :, pl.ds(y0, n)],
            dst_ref=raw.at[side, :, pl.ds(y0, n)],
            send_sem=xsend_sem.at[i],
            recv_sem=xrecv_sem.at[i],
            device_id=across,
            device_id_type=MESH,
        )

    def near_copy(src, y0, n, i):
        return pltpu.make_async_remote_copy(
            src_ref=src.at[:, pl.ds(y0, n)],
            dst_ref=raw.at[1, :, pl.ds(y0, n)],
            send_sem=nsend_sem.at[i],
            recv_sem=nrecv_sem.at[i],
            device_id=(twin, tm),
            device_id_type=MESH,
        )

    def far_copy(src, y0, n, i):
        return pltpu.make_async_remote_copy(
            src_ref=src.at[:, pl.ds(y0, n)],
            dst_ref=raw.at[0, :, pl.ds(y0, n)],
            send_sem=fsend_sem.at[i],
            recv_sem=frecv_sem.at[i],
            device_id=above,
            device_id_type=MESH,
        )

    def count_copy():
        return pltpu.make_async_remote_copy(
            src_ref=cnt.at[0],
            dst_ref=cnt.at[1],
            send_sem=csend_sem,
            recv_sem=crecv_sem,
            device_id=(twin, tm),
            device_id_type=MESH,
        )

    def red_copy(i):
        at = pl.ds(pl.multiple_of(i * 96, 96), 96)
        return pltpu.make_async_remote_copy(
            src_ref=rsend.at[at],
            dst_ref=rrecv.at[at],
            send_sem=rsend_sem.at[i],
            recv_sem=rrecv_sem.at[i],
            device_id=ahead,
            device_id_type=MESH,
        )

    def slot_of(d):
        return pl.ds(pl.multiple_of(d * lot, lot), lot)

    def send_copy(j, k):
        return pltpu.make_async_remote_copy(
            src_ref=psend.at[j],
            dst_ref=patches.at[j, slot_of(row)],
            send_sem=psend_sem.at[j, k],
            recv_sem=precv_sem.at[j, k],
            device_id=(lax.rem(dp + 2 * k, n_dp), across_tm),
            device_id_type=MESH,
        )

    def pass_copy(j, k):
        at = slot_of(lax.rem(home + n_dp - 2 * k, n_dp))
        return pltpu.make_async_remote_copy(
            src_ref=patches.at[j, at],
            dst_ref=patches.at[j, at],
            send_sem=gsend_sem.at[j, k],
            recv_sem=grecv_sem.at[j, k],
            device_id=(twin, tm),
            device_id_type=MESH,
        )

    def meta_copy(k):
        return pltpu.make_async_remote_copy(
            src_ref=meta,
            dst_ref=metas.at[dp],
            send_sem=msend_sem.at[k],
            recv_sem=mrecv_sem.at[k],
            device_id=(lax.rem(dp + k, n_dp), tm),
            device_id_type=MESH,
        )

    @pl.when(early)
    def _():
        for i in range(PIECES):
            cross_copy(*span(i), i).start()

    @pl.when(late)
    def _():
        load_own.start()

        @pl.when(side == 0)
        def _():
            for i in range(PIECES):
                near_copy(feat.at[0], *span(i), i).start()

        @pl.when((side == 1) & up)
        def _():
            for i in range(LEAD):
                far_copy(feat.at[0], *span(i), i).start()

    loads[0].wait()
    cnt[0] = jnp.zeros((8, 128), F32)
    cnt[0, 0:1, 0:videos] = counts[...].astype(F32)

    @pl.when(late)
    def _():
        count_copy().start()

    for load in loads[1:4]:
        load.wait()
    code = (owner[...] * pack + offset[...] + 1).astype(F32)
    named = jnp.concatenate(
        [code, bucket[...].astype(F32), jnp.zeros((6, rows), F32)], axis=0
    )
    frame = rows // 2
    meta[...] = jnp.concatenate(
        [
            named[:, f * frame + j * HALF : f * frame + j * HALF + HALF]
            for j in range(LOTS)
            for f in range(2)
        ],
        axis=1,
    )
    metas[dp] = meta[...]
    for k in range(1, n_dp):
        meta_copy(k).start()

    for field, side_len in ((p1, SIDE), (p2, HALF)):
        wide = field.shape[2]
        for s in range(4):
            field[s, :, 0:PAD] = jnp.zeros((side_len + 2, PAD, 128), F32)
            field[s, :, PAD + side_len : wide] = jnp.zeros((side_len + 2, PAD, 128), F32)
            field[s, 0] = jnp.zeros((wide, 128), F32)
            field[s, side_len + 1] = jnp.zeros((wide, 128), F32)

    @pl.when(jnp.logical_not(has_prev))
    def _():
        p1[0:2] = jnp.zeros((2,) + p1.shape[1:], F32)
        p2[0:2] = jnp.zeros((2,) + p2.shape[1:], F32)

    @pl.when(early)
    def _():
        count_copy().wait_recv()

    @pl.when(late)
    def _():
        cnt[1] = cnt[0]

    live = live_factors(cnt[1], slab * 2, videos)
    for load in loads[4:]:
        load.wait()
    for w, wm in ((w1, wm1), (w2, wm2)):
        wm[0, :, 0:128] = w[0] * live(0, 2)
        wm[1, :, 0:128] = w[1] * live(0, 1)
        wm[1, :, 128:256] = w[0] * live(1, 2)
        wm[2, :, 0:128] = w[2]
        wm[2, :, 128:256] = w[1] * live(1, 1)

    def mm(a, w):
        return jnp.dot(a, w, preferred_element_type=F32)

    def widen(pair, y0, n):
        for f in range(2):
            p1[2 * pair + f, pl.ds(1 + y0, n), PAD : PAD + SIDE, :] = raw[
                pair, f, pl.ds(y0, n)
            ].astype(F32)

    def take(y0, n, i):
        @pl.when(late)
        def _():
            cross_copy(y0, n, i).wait_recv()

            @pl.when((side == 0) & up)
            def _():
                far_copy(raw.at[1], y0, n, i).start()

            @pl.when(side == 1)
            def _():
                near_copy(raw.at[0], y0, n, i).start()

        @pl.when(early)
        def _():
            near_copy(raw.at[1], y0, n, i).wait_recv()

        @pl.when(down)
        def _():
            far_copy(raw.at[0], y0, n, i).wait_recv()

        widen(1, y0, n)

        @pl.when(has_prev)
        def _():
            widen(0, y0, n)

    def field1(s, y0):
        sides = []
        for parity in range(2):
            parts = []
            for dy in range(3):
                for dx in range(3):
                    v = p1[s, pl.ds(y0 + dy, 4), pl.ds(PAD + parity + dx - 1, 24, stride=2), :]
                    parts.append(v.reshape(96, 128).astype(BF16))
            sides.append(jnp.concatenate(parts, axis=1))
        return jnp.concatenate(sides, axis=0)

    def field2(s, y0):
        parts = []
        for dy in range(3):
            for dx in range(3):
                v = p2[s, pl.ds(y0 + dy, 4), PAD + dx - 1 : PAD + dx + 23, :]
                parts.append(v.reshape(96, 128).astype(BF16))
        return jnp.concatenate(parts, axis=1)

    def conv(field, y0, wm, w):
        both = mm(field(1, y0), wm[1]) + mm(field(2, y0), wm[2])
        ends = (mm(field(0, y0), wm[0, :, 0:128]), mm(field(3, y0), w[2]))
        return [both[:, f * 128 : f * 128 + 128] + ends[f] for f in range(2)]

    def section_one(i):
        y0 = 4 * i
        zs = conv(field1, y0, wm1, w1)
        blocks = []
        for f in range(2):
            z = (zs[f] + b1[...]).reshape(2, 2, 2, 24, 128)
            parts = {}
            for parity in range(2):
                x = p1[2 + f, pl.ds(1 + y0, 4), pl.ds(PAD + parity, 24, stride=2), :]
                x = x.reshape(2, 2, 24, 128)
                for by in range(2):
                    parts[by, parity] = (
                        (x[:, by] + silu(z[parity, :, by])).reshape(48, 128).astype(BF16)
                    )
            blocks.append(
                jnp.concatenate(
                    [parts[by, parity] for by in range(2) for parity in range(2)], axis=1
                )
            )
        red = (mm(jnp.concatenate(blocks, axis=0), sw[...]) + sb[...]).astype(BF16)
        rsend[pl.ds(pl.multiple_of(i * 96, 96), 96), :] = red

        @pl.when(has_next)
        def _():
            red_copy(i).start()

        wide = red.astype(F32).reshape(2, 2, 24, 128)
        for f in range(2):
            p2[2 + f, pl.ds(1 + 2 * i, 2), PAD : PAD + HALF, :] = wide[f]

    def take_red(i):
        red_copy(i).wait_recv()
        wide = rrecv[pl.ds(pl.multiple_of(i * 96, 96), 96), :].astype(F32)
        wide = wide.reshape(2, 2, 24, 128)
        for f in range(2):
            p2[f, pl.ds(1 + 2 * i, 2), PAD : PAD + HALF, :] = wide[f]

    def section_two(j):
        @pl.when(has_prev)
        def _():
            @pl.when(j == 0)
            def _():
                take_red(0)

            take_red(2 * j + 1)

            @pl.when(j < LOTS - 1)
            def _():
                take_red(2 * j + 2)

        y0 = 4 * j
        zs = conv(field2, y0, wm2, w2)
        for f in range(2):
            x = p2[2 + f, pl.ds(1 + y0, 4), PAD : PAD + HALF, :].reshape(96, 128)
            fs[f] = x + silu(zs[f] + b2[...])
            for b in range(2):
                for by in range(2):
                    for bx in range(2):
                        lane = (by * 2 + bx) * 128
                        to = f * 24 + b * 12
                        stage[to : to + 12, lane : lane + 128] = fs[
                            f, pl.ds(48 * b + 24 * by + bx, 12, stride=2), :
                        ]
        done = stage[...].astype(BF16)
        psend[j] = done
        for k in range(1, pairs):
            send_copy(j, k).start()

        @pl.when(core == 0)
        def _():
            send_copy(j, 0).start()

        @pl.when(core == 1)
        def _():
            patches[j, slot_of(home), :] = done
            pass_copy(j, 0).start()

    def hand_on(j):
        @pl.when(core == 0)
        def _():
            send_copy(j, 0).wait_recv()
            pass_copy(j, 0).start()

        for k in range(1, pairs):
            send_copy(j, k).wait_recv()
            pass_copy(j, k).start()

    def prepare():
        for k in range(1, n_dp):
            meta_copy(k).wait_recv()
        slot = lax.broadcasted_iota(jnp.int32, (pack, n_dp * lot), 0) + (dp * pack + 1)
        slot = slot.astype(F32)
        at = lax.broadcasted_iota(jnp.int32, (128, n_dp * lot), 0)
        name = lax.rem(at, names).astype(F32)
        inside = at < 3 * names
        sel = jnp.zeros((pack, 128), F32)
        for j in range(LOTS):
            both = jnp.concatenate(
                [metas[d, :, j * lot : j * lot + lot] for d in range(n_dp)], axis=1
            )
            marks = jnp.where(slot == both[0:1], 1.0, 0.0).astype(BF16)
            hot[j] = marks
            chosen = jnp.where((name == both[1:2]) & inside, 1.0, 0.0).astype(BF16)
            sel = sel + lax.dot_general(
                marks, chosen, (((1,), (1,)), ((), ())), preferred_element_type=F32
            )
        outv[:, 512:640] = sel.astype(BF16)

    @pl.when(late)
    def _():
        load_own.wait()

    sink = early & (side == 0)

    def arrive(j):
        for k in range(pairs):
            pass_copy(j, k).wait_recv()

    def advance(s, carry):
        @pl.when(s < STEPS)
        def _():
            @pl.when(s == 0)
            def _():
                take(*span(0), 0)

            @pl.when(s < STEPS - 1)
            def _():
                take(4 * s + 2, 4, s + 1)

            @pl.when(s == STEPS - 1)
            def _():
                take(*span(STEPS), STEPS)

            section_one(s)

        @pl.when(late & (s == STEPS))
        def _():
            prepare()

        def turn(start, by, fn):
            t = s - start
            ready = (t >= 0) & (t < by * LOTS) & (lax.rem(t + 2 * STEPS * by, by) == 0)

            @pl.when(ready)
            def _():
                fn(t // by)

        @pl.when((side == 1) & up)
        def _():
            @pl.when(s < STEPS - LEAD)
            def _():
                far_copy(feat.at[0], 4 * (s + LEAD) - 2, 4, s + LEAD).start()

            @pl.when(s == STEPS - LEAD)
            def _():
                far_copy(feat.at[0], *span(STEPS), STEPS).start()

        turn(3 + (2 * LAG - 1) * late_at, 2, section_two)
        turn(jnp.where(sink, 7, 40), 2, hand_on)
        return carry

    @pl.when(early)
    def _():
        prepare()

    lax.fori_loop(0, 20, advance, 0)

    def hand_on_late(lots):
        @pl.when(jnp.logical_not(sink))
        def _():
            for j in lots:
                hand_on(j)

    hand_on_late(range(LOTS - 2))
    for j in range(LOTS - 3):
        arrive(j)
    total = mm(hot[0], patches[0])
    for j in range(1, LOTS - 3):
        total = total + mm(hot[j], patches[j])
    got[...] = total
    for j in (LOTS - 3, LOTS - 2):
        hand_on_late((j + 1,))
        arrive(j)
        got[...] += mm(hot[j], patches[j])
    arrive(LOTS - 1)
    tile = pack // 2
    stores = []
    for m in range(2):
        at = pl.ds(m * tile, tile)
        rest = got[at] + mm(hot[LOTS - 1, at], patches[LOTS - 1])
        outv[at, 0:512] = rest.astype(BF16)
        stores.append(pltpu.make_async_copy(outv.at[at], out.at[at], out_sem.at[m]))
        stores[m].start()

    @pl.when(early)
    def _():
        for i in range(PIECES):
            cross_copy(*span(i), i).wait_send()

    @pl.when(late)
    def _():
        count_copy().wait_send()
        for i in range(PIECES):
            near_copy(raw.at[0], *span(i), i).wait_send()

    @pl.when(up)
    def _():
        for i in range(PIECES):
            far_copy(raw.at[1], *span(i), i).wait_send()

    @pl.when(core == 0)
    def _():
        for j in range(LOTS):
            send_copy(j, 0).wait_send()

    @pl.when(has_next)
    def _():
        for i in range(STEPS):
            red_copy(i).wait_send()

    for k in range(1, n_dp):
        meta_copy(k).wait_send()
    for j in range(LOTS):
        for k in range(1, pairs):
            send_copy(j, k).wait_send()
        for k in range(pairs):
            pass_copy(j, k).wait_send()
    for store in stores:
        store.wait()


def embed(packed, ew, eb, table, out, rows, out_sem):
    names = table.shape[0]
    full = table[...] + eb[...].reshape(1, -1)
    high = full.astype(BF16).astype(F32)
    mid = (full - high).astype(BF16).astype(F32)
    low = full - high - mid
    split = jnp.concatenate(
        [high, mid, low, jnp.zeros((128 - 3 * names, full.shape[1]), F32)], axis=0
    ).astype(BF16)
    tile = packed.shape[0] // TILES
    stores = []
    for m in range(TILES):
        at = pl.ds(m * tile, tile)
        total = jnp.dot(packed[at, 0:512], ew[...], preferred_element_type=F32)
        total = total + jnp.dot(packed[at, 512:640], split, preferred_element_type=F32)
        rows[at] = total.astype(BF16)
        stores.append(pltpu.make_async_copy(rows.at[at], out.at[at], out_sem.at[m]))
        stores[m].start()
    for store in stores:
        store.wait()


def shards(
    n_dp,
    n_tm,
    features,
    frame_counts,
    conv1_weight,
    conv1_bias,
    shrink_weight,
    shrink_bias,
    conv2_weight,
    conv2_bias,
    embed_weight,
    embed_bias,
    bucket_table,
    bucket_ids,
    dest_owner,
    dest_offset,
):
    rows = dest_owner.shape[1]
    pack = 2 * rows
    lat = embed_weight.shape[1]
    videos = frame_counts.shape[1]
    anywhere = pl.BlockSpec(memory_space=pl.ANY)
    pairs = n_dp // 2
    lot = 2 * HALF
    dma = pltpu.SemaphoreType.DMA
    gathered = pl.pallas_call(
        functools.partial(body, rows, pack, n_tm, n_dp, videos, bucket_table.shape[0]),
        out_shape=pltpu.VMEM((pack, 640), BF16),
        in_specs=[anywhere] * 11,
        out_specs=anywhere,
        scratch_shapes=[
            pltpu.VMEM((2, 2, SIDE, SIDE, 128), BF16),
            pltpu.VMEM((4, SIDE + 2, SIDE + 2 * PAD, 128), F32),
            pltpu.VMEM((4, HALF + 2, HALF + 2 * PAD, 128), F32),
            pltpu.VMEM((3, 1152, 128), BF16),
            pltpu.VMEM((3, 1152, 128), BF16),
            pltpu.VMEM((512, 128), BF16),
            pltpu.VMEM((1, videos), jnp.int32),
            pltpu.VMEM((1, 128), F32),
            pltpu.VMEM((1, 128), F32),
            pltpu.VMEM((1, 128), F32),
            pltpu.VMEM((1, rows), jnp.int32),
            pltpu.VMEM((1, rows), jnp.int32),
            pltpu.VMEM((1, rows), jnp.int32),
            pltpu.VMEM((3, 1152, 256), BF16),
            pltpu.VMEM((3, 1152, 256), BF16),
            pltpu.VMEM((2, 8, 128), F32),
            pltpu.VMEM((STEPS * 96, 128), BF16),
            pltpu.VMEM((STEPS * 96, 128), BF16),
            pltpu.VMEM((2, 96, 128), F32),
            pltpu.VMEM((lot, 512), F32),
            pltpu.VMEM((LOTS, lot, 512), BF16),
            pltpu.VMEM((LOTS, n_dp * lot, 512), BF16),
            pltpu.VMEM((8, rows), F32),
            pltpu.VMEM((n_dp, 8, rows), F32),
            pltpu.VMEM((LOTS, pack, n_dp * lot), BF16),
            pltpu.VMEM((pack, 512), F32),
            pltpu.VMEM((pack, 640), BF16),
            dma((10,)),
            dma,
            dma((2,)),
            dma,
            dma,
            dma((PIECES,)),
            dma((PIECES,)),
            dma((PIECES,)),
            dma((PIECES,)),
            dma((PIECES,)),
            dma((PIECES,)),
            dma((STEPS,)),
            dma((STEPS,)),
            dma((LOTS, pairs)),
            dma((LOTS, pairs)),
            dma((LOTS, pairs)),
            dma((LOTS, pairs)),
            dma((n_dp,)),
            dma((n_dp,)),
        ],
        compiler_params=pltpu.CompilerParams(
            collective_id=0, has_side_effects=True, vmem_limit_bytes=56 * 1024 * 1024
        ),
        name="encoder",
    )(
        features,
        frame_counts,
        conv1_weight.reshape(3, 1152, 128),
        conv1_bias.reshape(1, 128),
        shrink_weight,
        shrink_bias.reshape(1, 128),
        conv2_weight.reshape(3, 1152, 128),
        conv2_bias.reshape(1, 128),
        bucket_ids,
        dest_owner,
        dest_offset,
    )
    packed = pl.pallas_call(
        embed,
        out_shape=jax.ShapeDtypeStruct((pack, lat), BF16),
        in_specs=[pl.BlockSpec(memory_space=pltpu.VMEM)] * 4,
        out_specs=anywhere,
        scratch_shapes=[pltpu.VMEM((pack, lat), BF16), dma((TILES,))],
        compiler_params=pltpu.CompilerParams(vmem_limit_bytes=48 * 1024 * 1024),
        name="embed",
    )(gathered, embed_weight, embed_bias, bucket_table)
    return packed[None]


def solution(mesh):
    sizes = dict(mesh.shape)
    return jax.shard_map(
        functools.partial(shards, sizes["dp"], sizes["tm"]),
        mesh=mesh,
        in_specs=(
            P("dp", "tm", None, None, None),
            P("dp", None),
            P(),
            P(),
            P(),
            P(),
            P(),
            P(),
            P(),
            P(),
            P(),
            P("dp", "tm"),
            P("dp", "tm"),
            P("dp", "tm"),
        ),
        out_specs=P("dp", "tm", None),
        check_vma=False,
    )
```

```python
import functools
import jax
import jax.numpy as jnp
from jax import lax
from jax.experimental import pallas as pl
from jax.experimental.pallas import tpu as pltpu
from jax.sharding import PartitionSpec as P

MESH = pl.DeviceIdType.MESH
F32 = jnp.float32
BF16 = jnp.bfloat16
SIDE = 48
HALF = SIDE // 2
PAD = 8
STEPS = 12
PIECES = STEPS + 1
LOTS = 6
LAG = 3
LEAD = 4
TILES = 4


def silu(v):
    return v / (1.0 + jnp.exp(-v))


def span(i):
    return (0, 2) if i == 0 else (4 * i - 2, 2 if i == STEPS else 4)


def live_factors(counts, first, videos):
    def segment(moment):
        at = moment.astype(F32)
        total = jnp.zeros((1, 1), F32)
        bound = jnp.zeros((1, 1), F32)
        for i in range(videos):
            bound = bound + counts[0:1, i : i + 1]
            total = total + jnp.where(at >= bound, 1.0, 0.0)
        return total

    seg = {d: segment(first + d) for d in (-2, -1, 0, 1)}

    def live(frame, distance):
        same = jnp.where(seg[frame] == seg[frame - distance], 1.0, 0.0)
        there = jnp.where(first + frame - distance >= 0, 1.0, 0.0).astype(F32)
        return jnp.broadcast_to(same * there, (1, 128)).astype(BF16)

    return live


def body(
    rows,
    pack,
    n_tm,
    n_dp,
    videos,
    names,
    feat,
    counts_in,
    w1_in,
    b1_in,
    sw_in,
    sb_in,
    w2_in,
    b2_in,
    bucket_in,
    owner_in,
    offset_in,
    out,
    raw,
    p1,
    p2,
    w1,
    w2,
    sw,
    counts,
    b1,
    sb,
    b2,
    bucket,
    owner,
    offset,
    wm1,
    wm2,
    cnt,
    rsend,
    rrecv,
    fs,
    stage,
    psend,
    patches,
    meta,
    metas,
    hot,
    got,
    outv,
    load_sem,
    own_sem,
    out_sem,
    csend_sem,
    crecv_sem,
    xsend_sem,
    xrecv_sem,
    nsend_sem,
    nrecv_sem,
    fsend_sem,
    frecv_sem,
    rsend_sem,
    rrecv_sem,
    gsend_sem,
    grecv_sem,
    psend_sem,
    precv_sem,
    msend_sem,
    mrecv_sem,
):
    dp = lax.axis_index("dp")
    tm = lax.axis_index("tm")
    core = lax.rem(dp, 2)
    side = lax.rem(tm, 2)
    late = core == side
    early = core != side
    twin = dp + 1 - 2 * core
    across = (dp, tm + 1 - 2 * side)
    late_at = late.astype(jnp.int32)
    ahead = (twin, lax.rem(tm + 2 * late_at, n_tm))
    above = (twin, lax.rem(tm + 2, n_tm))
    below = (twin, lax.rem(tm + n_tm - 2, n_tm))
    row = dp - core + side
    slab = tm - side + late_at
    up = late & (tm < n_tm - 2)
    down = early & (tm > 1)
    has_next = early | up
    has_prev = late | down
    pairs = n_dp // 2
    home = dp - core + lax.rem(side + core + 1, 2)
    lot = 2 * HALF
    across_tm = jnp.where(core == 0, tm + 1 - 2 * side, tm)

    loads = [
        pltpu.make_async_copy(src, dst, load_sem.at[i])
        for i, (src, dst) in enumerate(
            (
                (counts_in, counts),
                (owner_in, owner),
                (offset_in, offset),
                (bucket_in, bucket),
                (w1_in, w1),
                (w2_in, w2),
                (sw_in, sw),
                (b1_in, b1),
                (sb_in, sb),
                (b2_in, b2),
            )
        )
    ]
    load_own = pltpu.make_async_copy(feat.at[0], raw.at[side], own_sem)

    barrier = pltpu.get_barrier_semaphore()
    for k in range(1, n_dp):
        pl.semaphore_signal(
            barrier, inc=1, device_id=(lax.rem(dp + k, n_dp), tm), device_id_type=MESH
        )

    pl.semaphore_signal(barrier, inc=1, device_id=across, device_id_type=MESH)

    @pl.when(core == 0)
    def _():
        for k in range(1, pairs):
            pl.semaphore_signal(
                barrier,
                inc=1,
                device_id=(lax.rem(dp + 2 * k, n_dp), across_tm),
                device_id_type=MESH,
            )

    @pl.when(up)
    def _():
        pl.semaphore_signal(barrier, inc=1, device_id=above, device_id_type=MESH)

    @pl.when(down)
    def _():
        pl.semaphore_signal(barrier, inc=1, device_id=below, device_id_type=MESH)

    for load in loads:
        load.start()
    links = up.astype(jnp.int32) + down.astype(jnp.int32)
    pl.semaphore_wait(barrier, n_dp + links + (1 - core) * (pairs - 1))

    def cross_copy(y0, n, i):
        return pltpu.make_async_remote_copy(
            src_ref=feat.at[0, :, pl.ds(y0, n)],
            dst_ref=raw.at[side, :, pl.ds(y0, n)],
            send_sem=xsend_sem.at[i],
            recv_sem=xrecv_sem.at[i],
            device_id=across,
            device_id_type=MESH,
        )

    def near_copy(src, y0, n, i):
        return pltpu.make_async_remote_copy(
            src_ref=src.at[:, pl.ds(y0, n)],
            dst_ref=raw.at[1, :, pl.ds(y0, n)],
            send_sem=nsend_sem.at[i],
            recv_sem=nrecv_sem.at[i],
            device_id=(twin, tm),
            device_id_type=MESH,
        )

    def far_copy(src, y0, n, i):
        return pltpu.make_async_remote_copy(
            src_ref=src.at[:, pl.ds(y0, n)],
            dst_ref=raw.at[0, :, pl.ds(y0, n)],
            send_sem=fsend_sem.at[i],
            recv_sem=frecv_sem.at[i],
            device_id=above,
            device_id_type=MESH,
        )

    def count_copy():
        return pltpu.make_async_remote_copy(
            src_ref=cnt.at[0],
            dst_ref=cnt.at[1],
            send_sem=csend_sem,
            recv_sem=crecv_sem,
            device_id=(twin, tm),
            device_id_type=MESH,
        )

    def red_copy(i):
        at = pl.ds(pl.multiple_of(i * 96, 96), 96)
        return pltpu.make_async_remote_copy(
            src_ref=rsend.at[at],
            dst_ref=rrecv.at[at],
            send_sem=rsend_sem.at[i],
            recv_sem=rrecv_sem.at[i],
            device_id=ahead,
            device_id_type=MESH,
        )

    def slot_of(d):
        return pl.ds(pl.multiple_of(d * lot, lot), lot)

    def send_copy(j, k):
        return pltpu.make_async_remote_copy(
            src_ref=psend.at[j],
            dst_ref=patches.at[j, slot_of(row)],
            send_sem=psend_sem.at[j, k],
            recv_sem=precv_sem.at[j, k],
            device_id=(lax.rem(dp + 2 * k, n_dp), across_tm),
            device_id_type=MESH,
        )

    def pass_copy(j, k):
        at = slot_of(lax.rem(home + n_dp - 2 * k, n_dp))
        return pltpu.make_async_remote_copy(
            src_ref=patches.at[j, at],
            dst_ref=patches.at[j, at],
            send_sem=gsend_sem.at[j, k],
            recv_sem=grecv_sem.at[j, k],
            device_id=(twin, tm),
            device_id_type=MESH,
        )

    def meta_copy(k):
        return pltpu.make_async_remote_copy(
            src_ref=meta,
            dst_ref=metas.at[dp],
            send_sem=msend_sem.at[k],
            recv_sem=mrecv_sem.at[k],
            device_id=(lax.rem(dp + k, n_dp), tm),
            device_id_type=MESH,
        )

    @pl.when(early)
    def _():
        for i in range(PIECES):
            cross_copy(*span(i), i).start()

    @pl.when(late)
    def _():
        load_own.start()

        @pl.when(side == 0)
        def _():
            for i in range(PIECES):
                near_copy(feat.at[0], *span(i), i).start()

        @pl.when((side == 1) & up)
        def _():
            for i in range(LEAD):
                far_copy(feat.at[0], *span(i), i).start()

    loads[0].wait()
    cnt[0] = jnp.zeros((8, 128), F32)
    cnt[0, 0:1, 0:videos] = counts[...].astype(F32)

    @pl.when(late)
    def _():
        count_copy().start()

    for load in loads[1:4]:
        load.wait()
    code = (owner[...] * pack + offset[...] + 1).astype(F32)
    named = jnp.concatenate(
        [code, bucket[...].astype(F32), jnp.zeros((6, rows), F32)], axis=0
    )
    frame = rows // 2
    meta[...] = jnp.concatenate(
        [
            named[:, f * frame + j * HALF : f * frame + j * HALF + HALF]
            for j in range(LOTS)
            for f in range(2)
        ],
        axis=1,
    )
    metas[dp] = meta[...]
    for k in range(1, n_dp):
        meta_copy(k).start()

    for field, side_len in ((p1, SIDE), (p2, HALF)):
        wide = field.shape[2]
        for s in range(4):
            field[s, :, 0:PAD] = jnp.zeros((side_len + 2, PAD, 128), F32)
            field[s, :, PAD + side_len : wide] = jnp.zeros((side_len + 2, PAD, 128), F32)
            field[s, 0] = jnp.zeros((wide, 128), F32)
            field[s, side_len + 1] = jnp.zeros((wide, 128), F32)

    @pl.when(jnp.logical_not(has_prev))
    def _():
        p1[0:2] = jnp.zeros((2,) + p1.shape[1:], F32)
        p2[0:2] = jnp.zeros((2,) + p2.shape[1:], F32)

    @pl.when(early)
    def _():
        count_copy().wait_recv()

    @pl.when(late)
    def _():
        cnt[1] = cnt[0]

    live = live_factors(cnt[1], slab * 2, videos)
    for load in loads[4:]:
        load.wait()
    for w, wm in ((w1, wm1), (w2, wm2)):
        wm[0, :, 0:128] = w[0] * live(0, 2)
        wm[1, :, 0:128] = w[1] * live(0, 1)
        wm[1, :, 128:256] = w[0] * live(1, 2)
        wm[2, :, 0:128] = w[2]
        wm[2, :, 128:256] = w[1] * live(1, 1)

    def mm(a, w):
        return jnp.dot(a, w, preferred_element_type=F32)

    def widen(pair, y0, n):
        for f in range(2):
            p1[2 * pair + f, pl.ds(1 + y0, n), PAD : PAD + SIDE, :] = raw[
                pair, f, pl.ds(y0, n)
            ].astype(F32)

    def take(y0, n, i):
        @pl.when(late)
        def _():
            cross_copy(y0, n, i).wait_recv()

            @pl.when((side == 0) & up)
            def _():
                far_copy(raw.at[1], y0, n, i).start()

            @pl.when(side == 1)
            def _():
                near_copy(raw.at[0], y0, n, i).start()

        @pl.when(early)
        def _():
            near_copy(raw.at[1], y0, n, i).wait_recv()

        @pl.when(down)
        def _():
            far_copy(raw.at[0], y0, n, i).wait_recv()

        widen(1, y0, n)

        @pl.when(has_prev)
        def _():
            widen(0, y0, n)

    def field1(s, y0):
        sides = []
        for parity in range(2):
            parts = []
            for dy in range(3):
                for dx in range(3):
                    v = p1[s, pl.ds(y0 + dy, 4), pl.ds(PAD + parity + dx - 1, 24, stride=2), :]
                    parts.append(v.reshape(96, 128).astype(BF16))
            sides.append(jnp.concatenate(parts, axis=1))
        return jnp.concatenate(sides, axis=0)

    def field2(s, y0):
        parts = []
        for dy in range(3):
            for dx in range(3):
                v = p2[s, pl.ds(y0 + dy, 4), PAD + dx - 1 : PAD + dx + 23, :]
                parts.append(v.reshape(96, 128).astype(BF16))
        return jnp.concatenate(parts, axis=1)

    def conv(field, y0, wm, w):
        both = mm(field(1, y0), wm[1]) + mm(field(2, y0), wm[2])
        ends = (mm(field(0, y0), wm[0, :, 0:128]), mm(field(3, y0), w[2]))
        return [both[:, f * 128 : f * 128 + 128] + ends[f] for f in range(2)]

    def section_one(i):
        y0 = 4 * i
        zs = conv(field1, y0, wm1, w1)
        blocks = []
        for f in range(2):
            z = (zs[f] + b1[...]).reshape(2, 2, 2, 24, 128)
            parts = {}
            for parity in range(2):
                x = p1[2 + f, pl.ds(1 + y0, 4), pl.ds(PAD + parity, 24, stride=2), :]
                x = x.reshape(2, 2, 24, 128)
                for by in range(2):
                    parts[by, parity] = (
                        (x[:, by] + silu(z[parity, :, by])).reshape(48, 128).astype(BF16)
                    )
            blocks.append(
                jnp.concatenate(
                    [parts[by, parity] for by in range(2) for parity in range(2)], axis=1
                )
            )
        red = (mm(jnp.concatenate(blocks, axis=0), sw[...]) + sb[...]).astype(BF16)
        rsend[pl.ds(pl.multiple_of(i * 96, 96), 96), :] = red

        @pl.when(has_next)
        def _():
            red_copy(i).start()

        wide = red.astype(F32).reshape(2, 2, 24, 128)
        for f in range(2):
            p2[2 + f, pl.ds(1 + 2 * i, 2), PAD : PAD + HALF, :] = wide[f]

    def take_red(i):
        red_copy(i).wait_recv()
        wide = rrecv[pl.ds(pl.multiple_of(i * 96, 96), 96), :].astype(F32)
        wide = wide.reshape(2, 2, 24, 128)
        for f in range(2):
            p2[f, pl.ds(1 + 2 * i, 2), PAD : PAD + HALF, :] = wide[f]

    def section_two(j):
        @pl.when(has_prev)
        def _():
            @pl.when(j == 0)
            def _():
                take_red(0)

            take_red(2 * j + 1)

            @pl.when(j < LOTS - 1)
            def _():
                take_red(2 * j + 2)

        y0 = 4 * j
        zs = conv(field2, y0, wm2, w2)
        for f in range(2):
            x = p2[2 + f, pl.ds(1 + y0, 4), PAD : PAD + HALF, :].reshape(96, 128)
            fs[f] = x + silu(zs[f] + b2[...])
            for b in range(2):
                for by in range(2):
                    for bx in range(2):
                        lane = (by * 2 + bx) * 128
                        to = f * 24 + b * 12
                        stage[to : to + 12, lane : lane + 128] = fs[
                            f, pl.ds(48 * b + 24 * by + bx, 12, stride=2), :
                        ]
        done = stage[...].astype(BF16)
        psend[j] = done
        for k in range(1, pairs):
            send_copy(j, k).start()

        @pl.when(core == 0)
        def _():
            send_copy(j, 0).start()

        @pl.when(core == 1)
        def _():
            patches[j, slot_of(home), :] = done
            pass_copy(j, 0).start()

    def hand_on(j):
        @pl.when(core == 0)
        def _():
            send_copy(j, 0).wait_recv()
            pass_copy(j, 0).start()

        for k in range(1, pairs):
            send_copy(j, k).wait_recv()
            pass_copy(j, k).start()

    def prepare():
        for k in range(1, n_dp):
            meta_copy(k).wait_recv()
        slot = lax.broadcasted_iota(jnp.int32, (pack, n_dp * lot), 0) + (dp * pack + 1)
        slot = slot.astype(F32)
        at = lax.broadcasted_iota(jnp.int32, (128, n_dp * lot), 0)
        name = lax.rem(at, names).astype(F32)
        inside = at < 3 * names
        sel = jnp.zeros((pack, 128), F32)
        for j in range(LOTS):
            both = jnp.concatenate(
                [metas[d, :, j * lot : j * lot + lot] for d in range(n_dp)], axis=1
            )
            marks = jnp.where(slot == both[0:1], 1.0, 0.0).astype(BF16)
            hot[j] = marks
            chosen = jnp.where((name == both[1:2]) & inside, 1.0, 0.0).astype(BF16)
            sel = sel + lax.dot_general(
                marks, chosen, (((1,), (1,)), ((), ())), preferred_element_type=F32
            )
        outv[:, 512:640] = sel.astype(BF16)

    @pl.when(late)
    def _():
        load_own.wait()

    sink = early & (side == 0)

    def arrive(j):
        for k in range(pairs):
            pass_copy(j, k).wait_recv()

    def advance(s, carry):
        @pl.when(s < STEPS)
        def _():
            @pl.when(s == 0)
            def _():
                take(*span(0), 0)

            @pl.when(s < STEPS - 1)
            def _():
                take(4 * s + 2, 4, s + 1)

            @pl.when(s == STEPS - 1)
            def _():
                take(*span(STEPS), STEPS)

            section_one(s)

        @pl.when(late & (s == STEPS))
        def _():
            prepare()

        def turn(start, by, fn):
            t = s - start
            ready = (t >= 0) & (t < by * LOTS) & (lax.rem(t + 2 * STEPS * by, by) == 0)

            @pl.when(ready)
            def _():
                fn(t // by)

        @pl.when((side == 1) & up)
        def _():
            @pl.when(s < STEPS - LEAD)
            def _():
                far_copy(feat.at[0], 4 * (s + LEAD) - 2, 4, s + LEAD).start()

            @pl.when(s == STEPS - LEAD)
            def _():
                far_copy(feat.at[0], *span(STEPS), STEPS).start()

        turn(3 + (2 * LAG - 1) * late_at, 2, section_two)
        turn(jnp.where(sink, 7, 40), 2, hand_on)
        return carry

    @pl.when(early)
    def _():
        prepare()

    lax.fori_loop(0, 20, advance, 0)

    def hand_on_late(lots):
        @pl.when(jnp.logical_not(sink))
        def _():
            for j in lots:
                hand_on(j)

    hand_on_late(range(LOTS - 2))
    for j in range(LOTS - 3):
        arrive(j)
    total = mm(hot[0], patches[0])
    for j in range(1, LOTS - 3):
        total = total + mm(hot[j], patches[j])
    got[...] = total
    for j in (LOTS - 3, LOTS - 2):
        hand_on_late((j + 1,))
        arrive(j)
        got[...] += mm(hot[j], patches[j])
    arrive(LOTS - 1)
    tile = pack // 2
    stores = []
    for m in range(2):
        at = pl.ds(m * tile, tile)
        rest = got[at] + mm(hot[LOTS - 1, at], patches[LOTS - 1])
        outv[at, 0:512] = rest.astype(BF16)
        stores.append(pltpu.make_async_copy(outv.at[at], out.at[at], out_sem.at[m]))
        stores[m].start()

    @pl.when(early)
    def _():
        for i in range(PIECES):
            cross_copy(*span(i), i).wait_send()

    @pl.when(late)
    def _():
        count_copy().wait_send()
        for i in range(PIECES):
            near_copy(raw.at[0], *span(i), i).wait_send()

    @pl.when(up)
    def _():
        for i in range(PIECES):
            far_copy(raw.at[1], *span(i), i).wait_send()

    @pl.when(core == 0)
    def _():
        for j in range(LOTS):
            send_copy(j, 0).wait_send()

    @pl.when(has_next)
    def _():
        for i in range(STEPS):
            red_copy(i).wait_send()

    for k in range(1, n_dp):
        meta_copy(k).wait_send()
    for j in range(LOTS):
        for k in range(1, pairs):
            send_copy(j, k).wait_send()
        for k in range(pairs):
            pass_copy(j, k).wait_send()
    for store in stores:
        store.wait()


def embed(packed, ew, eb, table, out, rows, out_sem):
    names = table.shape[0]
    full = table[...] + eb[...].reshape(1, -1)
    high = full.astype(BF16).astype(F32)
    mid = (full - high).astype(BF16).astype(F32)
    low = full - high - mid
    split = jnp.concatenate(
        [high, mid, low, jnp.zeros((128 - 3 * names, full.shape[1]), F32)], axis=0
    ).astype(BF16)
    tile = packed.shape[0] // TILES
    stores = []
    for m in range(TILES):
        at = pl.ds(m * tile, tile)
        total = jnp.dot(packed[at, 0:512], ew[...], preferred_element_type=F32)
        total = total + jnp.dot(packed[at, 512:640], split, preferred_element_type=F32)
        rows[at] = total.astype(BF16)
        stores.append(pltpu.make_async_copy(rows.at[at], out.at[at], out_sem.at[m]))
        stores[m].start()
    for store in stores:
        store.wait()


def shards(
    n_dp,
    n_tm,
    features,
    frame_counts,
    conv1_weight,
    conv1_bias,
    shrink_weight,
    shrink_bias,
    conv2_weight,
    conv2_bias,
    embed_weight,
    embed_bias,
    bucket_table,
    bucket_ids,
    dest_owner,
    dest_offset,
):
    rows = dest_owner.shape[1]
    pack = 2 * rows
    lat = embed_weight.shape[1]
    videos = frame_counts.shape[1]
    anywhere = pl.BlockSpec(memory_space=pl.ANY)
    pairs = n_dp // 2
    lot = 2 * HALF
    dma = pltpu.SemaphoreType.DMA
    gathered = pl.pallas_call(
        functools.partial(body, rows, pack, n_tm, n_dp, videos, bucket_table.shape[0]),
        out_shape=pltpu.VMEM((pack, 640), BF16),
        in_specs=[anywhere] * 11,
        out_specs=anywhere,
        scratch_shapes=[
            pltpu.VMEM((2, 2, SIDE, SIDE, 128), BF16),
            pltpu.VMEM((4, SIDE + 2, SIDE + 2 * PAD, 128), F32),
            pltpu.VMEM((4, HALF + 2, HALF + 2 * PAD, 128), F32),
            pltpu.VMEM((3, 1152, 128), BF16),
            pltpu.VMEM((3, 1152, 128), BF16),
            pltpu.VMEM((512, 128), BF16),
            pltpu.VMEM((1, videos), jnp.int32),
            pltpu.VMEM((1, 128), F32),
            pltpu.VMEM((1, 128), F32),
            pltpu.VMEM((1, 128), F32),
            pltpu.VMEM((1, rows), jnp.int32),
            pltpu.VMEM((1, rows), jnp.int32),
            pltpu.VMEM((1, rows), jnp.int32),
            pltpu.VMEM((3, 1152, 256), BF16),
            pltpu.VMEM((3, 1152, 256), BF16),
            pltpu.VMEM((2, 8, 128), F32),
            pltpu.VMEM((STEPS * 96, 128), BF16),
            pltpu.VMEM((STEPS * 96, 128), BF16),
            pltpu.VMEM((2, 96, 128), F32),
            pltpu.VMEM((lot, 512), F32),
            pltpu.VMEM((LOTS, lot, 512), BF16),
            pltpu.VMEM((LOTS, n_dp * lot, 512), BF16),
            pltpu.VMEM((8, rows), F32),
            pltpu.VMEM((n_dp, 8, rows), F32),
            pltpu.VMEM((LOTS, pack, n_dp * lot), BF16),
            pltpu.VMEM((pack, 512), F32),
            pltpu.VMEM((pack, 640), BF16),
            dma((10,)),
            dma,
            dma((2,)),
            dma,
            dma,
            dma((PIECES,)),
            dma((PIECES,)),
            dma((PIECES,)),
            dma((PIECES,)),
            dma((PIECES,)),
            dma((PIECES,)),
            dma((STEPS,)),
            dma((STEPS,)),
            dma((LOTS, pairs)),
            dma((LOTS, pairs)),
            dma((LOTS, pairs)),
            dma((LOTS, pairs)),
            dma((n_dp,)),
            dma((n_dp,)),
        ],
        compiler_params=pltpu.CompilerParams(
            collective_id=0, has_side_effects=True, vmem_limit_bytes=56 * 1024 * 1024
        ),
        name="encoder",
    )(
        features,
        frame_counts,
        conv1_weight.reshape(3, 1152, 128),
        conv1_bias.reshape(1, 128),
        shrink_weight,
        shrink_bias.reshape(1, 128),
        conv2_weight.reshape(3, 1152, 128),
        conv2_bias.reshape(1, 128),
        bucket_ids,
        dest_owner,
        dest_offset,
    )
    packed = pl.pallas_call(
        embed,
        out_shape=jax.ShapeDtypeStruct((pack, lat), BF16),
        in_specs=[pl.BlockSpec(memory_space=pltpu.VMEM)] * 4,
        out_specs=anywhere,
        scratch_shapes=[pltpu.VMEM((pack, lat), BF16), dma((TILES,))],
        compiler_params=pltpu.CompilerParams(vmem_limit_bytes=48 * 1024 * 1024),
        name="embed",
    )(gathered, embed_weight, embed_bias, bucket_table)
    return packed[None]


def solution(mesh):
    sizes = dict(mesh.shape)
    return jax.shard_map(
        functools.partial(shards, sizes["dp"], sizes["tm"]),
        mesh=mesh,
        in_specs=(
            P("dp", "tm", None, None, None),
            P("dp", None),
            P(),
            P(),
            P(),
            P(),
            P(),
            P(),
            P(),
            P(),
            P(),
            P("dp", "tm"),
            P("dp", "tm"),
            P("dp", "tm"),
        ),
        out_specs=P("dp", "tm", None),
        check_vma=False,
    )
```
